256 devices in a mesh: date: 32 (over z, y_lo, core), strip: 8 (over x, y_hi).
Axes of the slice: x: 4, y: 4 (y_hi: 2, y_lo: 2; y = y_hi * 2 + y_lo), z: 8, core: 2. Of those that a mesh axis runs over, the one named last changes fastest.
Arguments:
- acquisitions: bfloat16 [64, 2, 2, 344, 2560], P('date', None, None, None, 'strip'), may hold values from -6 to 6
- shifts: int32 [2, 64, 2, 5, 40], P(None, 'date', None, None, 'strip'), may hold values from -8 to 8, as said below
- fractions: int32 [2, 64, 2, 5, 40], P(None, 'date', None, None, 'strip'), may hold values from 0 to 63
- ref_dates: int32 [2], replicated, may hold values from 0 to 63, as said below
Outputs:
- chip_corr: float32 [2, 64, 2, 5, 40], P(None, 'date', None, None, 'strip')
- coherence: float32 [2, 63, 2, 64, 128], P(None, None, None, 'date', 'strip')
The draws below stay inside these ranges and needn't reach their ends.
Inputs may be any that keep to these rules, and one draw needn't show every extreme that they name: `shifts`: zero at every chip of date ref_dates[t] in tile t. `ref_dates`: the reference dates of consecutive tiles lie in different blocks of 2 dates.
All inputs are finite; a program needn't handle non-finite values.
Results may differ from the reference program's by a relative error of at most 0.0021.
Values may be sent and summed in bfloat16 or wider, within the bound.
No kernel may reach another device: no remote copies, remote signals or barrier semaphores. Data moves between devices by JAX's collectives and lax.ppermute only.
A program may use at most 64 MiB of HBM per device.

```python
import jax
import jax.numpy as jnp
from jax import lax

DATE_DEV = 2
TILE_COUNT = 2
TILE_ROWS = 320
CHIP_SIZE = 64
MAX_SHIFT = 8
TAP_COUNT = 8
SUBSTEPS = 64
LOOK_AZ = 5
LOOK_RG = 20
DATE_COUNT = 64
TILE_COLS = 2560
MARGIN = 12
CHIPS_AZ = 5
CHIPS_RG = 40
PAIR_COUNT = 63


def draw_layout(key):
    keys = jax.random.split(jax.random.fold_in(key, 11), 6)
    device_count = DATE_COUNT // DATE_DEV
    first_owner = jax.random.randint(keys[0], (), 0, device_count)
    stride = jax.random.randint(keys[1], (), 1, device_count)
    end_tile = jax.random.randint(keys[5], (), 0, TILE_COUNT)
    tile_axis = jnp.arange(TILE_COUNT, dtype=jnp.int32)
    base_owners = (first_owner + tile_axis * stride) % device_count
    owners = (base_owners - base_owners[end_tile] + device_count - 1) % device_count
    slot_pick = jax.random.randint(keys[2], (TILE_COUNT,), 0, DATE_DEV)
    slot_pick = jnp.where(tile_axis == end_tile, DATE_DEV - 1, slot_pick)
    ref_dates = (owners * DATE_DEV + slot_pick).astype(jnp.int32)
    baseline = jax.random.randint(keys[3], (2, DATE_COUNT, TILE_COUNT, 1, 1), 2 - MAX_SHIFT, MAX_SHIFT - 1)
    jitter = jax.random.randint(keys[4], (2, DATE_COUNT, TILE_COUNT, CHIPS_AZ, CHIPS_RG), -2, 3)
    is_reference = jnp.arange(DATE_COUNT, dtype=jnp.int32)[:, None] == ref_dates[None, :]
    shifts = jnp.where(is_reference[None, :, :, None, None], 0, baseline + jitter)
    return (ref_dates, shifts.astype(jnp.int32))


def draw_ref_dates(key, part):
    return draw_layout(key)[0]


def draw_shifts(key, part):
    return draw_layout(key)[1]


def draw_acquisitions(key, part):
    ref_dates, shifts = draw_layout(key)
    scene_key, noise_key = jax.random.split(jax.random.fold_in(key, 23))
    scene_shape = (TILE_COUNT, 2, TILE_ROWS + 2 * MARGIN + 2 * MAX_SHIFT, TILE_COLS + 2 * MAX_SHIFT)
    scene = jax.random.normal(scene_key, scene_shape, jnp.float32)
    line_rows = jnp.arange(TILE_ROWS + 2 * MARGIN, dtype=jnp.int32)
    line_cols = jnp.arange(TILE_COLS, dtype=jnp.int32)
    chip_rows = jnp.clip((line_rows - MARGIN) // CHIP_SIZE, 0, CHIPS_AZ - 1)
    chip_cols = line_cols // CHIP_SIZE
    tile_axis = jnp.arange(TILE_COUNT, dtype=jnp.int32)[:, None, None, None]
    part_axis = jnp.arange(2, dtype=jnp.int32)[None, :, None, None]

    def one_date(date_index):
        offsets = -lax.dynamic_index_in_dim(shifts, date_index, 1, keepdims=False)
        row_offsets = offsets[0][:, chip_rows[:, None], chip_cols[None, :]]
        col_offsets = offsets[1][:, chip_rows[:, None], chip_cols[None, :]]
        source_rows = line_rows[None, :, None] + row_offsets + MAX_SHIFT
        source_cols = line_cols[None, None, :] + col_offsets + MAX_SHIFT
        values = scene[tile_axis, part_axis, source_rows[:, None], source_cols[:, None]]
        date_key = jax.random.fold_in(noise_key, date_index)
        noise = 0.5 * jax.random.normal(date_key, values.shape, jnp.float32)
        return jnp.clip(values + noise, -6.0, 6.0)
    return lax.map(one_date, jnp.arange(DATE_COUNT, dtype=jnp.int32)).astype(jnp.bfloat16)


def touch_ends(drawn, rng, low, top_value):
    longest = drawn.shape.index(max(drawn.shape))
    spots = []
    for shift in (0, 1):
        where = [jax.random.randint(jax.random.fold_in(rng, axis), (), 0, length) for axis, length in enumerate(drawn.shape)]
        where[longest] = (where[longest] + shift) % drawn.shape[longest]
        spots.append(tuple(where))
    return drawn.at[spots[0]].set(low).at[spots[1]].set(top_value)


def setup_inputs(seed: int = 0) -> dict:
    streams_of = jax.random.split(jax.random.key(seed), 5)
    return {
        "acquisitions": draw_acquisitions(jax.random.fold_in(streams_of[4], 71), 0),
        "shifts": draw_shifts(jax.random.fold_in(streams_of[4], 71), 0),
        "fractions": touch_ends(jax.random.randint(streams_of[2], (2, DATE_COUNT, TILE_COUNT, CHIPS_AZ, CHIPS_RG), 0, SUBSTEPS), jax.random.fold_in(streams_of[2], 1), 0, SUBSTEPS - 1).astype(jnp.int32),
        "ref_dates": draw_ref_dates(jax.random.fold_in(streams_of[4], 71), 0),
    }


epsilon = 1e-06

def sinc_matrix(shift_part, fraction_part):
    window_size = CHIP_SIZE + 2 * MARGIN
    offset = fraction_part.astype(jnp.float32) / SUBSTEPS
    tap_axis = jnp.arange(TAP_COUNT).astype(jnp.float32)
    distance = tap_axis - (TAP_COUNT // 2 - 1) - offset[..., None]
    weights = jnp.sinc(distance) * (0.5 + 0.5 * jnp.cos(jnp.pi * distance / (TAP_COUNT // 2)))
    weights = weights / lax.optimization_barrier(jnp.sum(weights, axis=-1, keepdims=True))
    out_rows = jnp.arange(CHIP_SIZE, dtype=jnp.int32)[:, None]
    in_rows = jnp.arange(window_size, dtype=jnp.int32)[None, :]
    matrix = jnp.zeros(shift_part.shape + (CHIP_SIZE, window_size), jnp.float32)
    for tap_index in range(TAP_COUNT):
        target = out_rows + shift_part[..., None, None] + (tap_index - TAP_COUNT // 2 + 1 + MARGIN)
        matrix = matrix + jnp.where(in_rows == target, weights[..., tap_index][..., None, None], 0.0)
    return matrix.astype(jnp.bfloat16)

def correlate(reference_tiles, resampled):
    chips_az = resampled.shape[-2] // CHIP_SIZE
    chips_rg = resampled.shape[-1] // CHIP_SIZE

    def as_chips(values):
        return values.astype(jnp.float32).reshape(values.shape[:-2] + (chips_az, CHIP_SIZE, chips_rg, CHIP_SIZE))
    ref_chips = as_chips(reference_tiles)
    sec_chips = as_chips(resampled)
    ref_real = ref_chips[..., 0, :, :, :, :]
    ref_imag = ref_chips[..., 1, :, :, :, :]
    sec_real = sec_chips[..., 0, :, :, :, :]
    sec_imag = sec_chips[..., 1, :, :, :, :]
    cross_real = lax.optimization_barrier(jnp.sum(ref_real * sec_real + ref_imag * sec_imag, axis=(-3, -1)))
    cross_imag = lax.optimization_barrier(jnp.sum(ref_imag * sec_real - ref_real * sec_imag, axis=(-3, -1)))
    ref_power = lax.optimization_barrier(jnp.sum(ref_real * ref_real + ref_imag * ref_imag, axis=(-3, -1)))
    sec_power = lax.optimization_barrier(jnp.sum(sec_real * sec_real + sec_imag * sec_imag, axis=(-3, -1)))
    denominator = jnp.sqrt((ref_power + epsilon) * (sec_power + epsilon))
    return jnp.stack([cross_real / denominator, cross_imag / denominator])

def multilook_pairs(series):
    values = series.astype(jnp.float32)
    earlier = values[:-1]
    second = values[1:]
    early_real = earlier[:, :, 0]
    early_imag = earlier[:, :, 1]
    later_real = second[:, :, 0]
    later_imag = second[:, :, 1]
    cross_real = early_real * later_real + early_imag * later_imag
    cross_imag = early_imag * later_real - early_real * later_imag
    power_early = early_real * early_real + early_imag * early_imag
    power_later = later_real * later_real + later_imag * later_imag

    def box_sum(quantity):
        blocked = quantity.reshape(quantity.shape[:2] + (quantity.shape[2] // LOOK_AZ, LOOK_AZ, quantity.shape[3] // LOOK_RG, LOOK_RG))
        return lax.optimization_barrier(jnp.sum(blocked, axis=(3, 5)))
    denominator = jnp.sqrt((box_sum(power_early) + epsilon) * (box_sum(power_later) + epsilon))
    return jnp.stack([box_sum(cross_real) / denominator, box_sum(cross_imag) / denominator])

def reference(acquisitions, shifts, fractions, ref_dates):
    window_size = CHIP_SIZE + 2 * MARGIN
    padded = jnp.pad(acquisitions, ((0, 0), (0, 0), (0, 0), (0, 0), (MARGIN, MARGIN)))
    reference_tiles = jnp.stack([lax.dynamic_index_in_dim(acquisitions[:, tile_index], ref_dates[tile_index], 0, keepdims=False)[:, MARGIN:MARGIN + TILE_ROWS, :] for tile_index in range(TILE_COUNT)])
    row_index = (jnp.arange(CHIPS_AZ, dtype=jnp.int32) * CHIP_SIZE)[:, None] + jnp.arange(window_size, dtype=jnp.int32)[None, :]
    col_index = (jnp.arange(CHIPS_RG, dtype=jnp.int32) * CHIP_SIZE)[:, None] + jnp.arange(window_size, dtype=jnp.int32)[None, :]

    def one_date(date_index):
        date_frame = lax.dynamic_index_in_dim(padded, date_index, 0, keepdims=False)
        windows = date_frame[:, :, row_index[:, :, None, None], col_index[None, None, :, :]]
        windows = windows.transpose(0, 2, 4, 1, 3, 5).astype(jnp.float32)
        shift_now = lax.dynamic_index_in_dim(shifts, date_index, 1, keepdims=False)
        fraction_now = lax.dynamic_index_in_dim(fractions, date_index, 1, keepdims=False)
        azimuth = sinc_matrix(shift_now[0], fraction_now[0]).astype(jnp.float32)
        across = sinc_matrix(shift_now[1], fraction_now[1]).astype(jnp.float32)
        partial_rows = jnp.einsum('tariw,tarcwv->tarciv', azimuth, windows).astype(jnp.bfloat16)
        chips_out = jnp.einsum('tarciv,tarjv->tarcij', partial_rows.astype(jnp.float32), across).astype(jnp.bfloat16)
        resampled = chips_out.transpose(0, 3, 1, 4, 2, 5).reshape(TILE_COUNT, 2, TILE_ROWS, TILE_COLS)
        return (resampled, correlate(reference_tiles, resampled))
    resampled_all, corr_all = lax.map(one_date, jnp.arange(DATE_COUNT, dtype=jnp.int32))
    chip_corr = corr_all.transpose(1, 0, 2, 3, 4)

    def one_pair(pair_index):
        couple = lax.dynamic_slice_in_dim(resampled_all, pair_index, 2, 0)
        return multilook_pairs(couple)[:, 0]
    looked = lax.map(one_pair, jnp.arange(PAIR_COUNT, dtype=jnp.int32))
    coherence = looked.transpose(1, 0, 2, 3, 4)
    return (chip_corr, coherence)
```

```python
import functools

import jax
import jax.numpy as jnp
import numpy as np
from jax import lax
from jax.experimental import pallas as pl
from jax.experimental.pallas import tpu as pltpu
from jax.sharding import PartitionSpec as P

CHIP = 64
TAPS = 8
SUBSTEPS = 64
LOOK_AZ = 5
LOOK_RG = 20
MARGIN = 12
WINDOW = CHIP + 2 * MARGIN
LANES = 128
EDGE = 16
UNROLL = 1
EPSILON = 1e-06

VMEM = pl.BlockSpec(memory_space=pltpu.VMEM)
SMEM = pl.BlockSpec(memory_space=pltpu.SMEM)
F32 = jnp.float32
BF16 = jnp.bfloat16


def tap_table():
    x = np.arange(TAPS)[None, :] - (TAPS // 2 - 1) - np.arange(SUBSTEPS)[:, None] / SUBSTEPS
    weights = np.sinc(x) * (0.5 + 0.5 * np.cos(2 * np.pi * x / TAPS))
    weights = weights / weights.sum(axis=1, keepdims=True)
    table = np.zeros((SUBSTEPS, CHIP, LANES), np.float32)
    for line in range(CHIP):
        table[:, line, line : line + TAPS] = weights
    return table.astype(jnp.bfloat16)


def look_matrices(lines):
    chips = lines // CHIP
    looks = lines // LOOK_AZ
    plain = np.zeros((looks, chips, 2, CHIP), np.float32)
    for line in range(lines):
        plain[line // LOOK_AZ, line // CHIP, :, line % CHIP] = 1.0
    signed = plain.copy()
    signed[:, :, 1] *= -1.0
    return [m.reshape(looks, chips * LANES).astype(jnp.bfloat16) for m in (plain, signed)]


def lane_index(shape):
    return lax.broadcasted_iota(jnp.int32, shape, len(shape) - 1)


def call(body, outs, in_specs, scratch=(), cost=(0, 0)):
    return pl.pallas_call(
        body,
        out_shape=outs,
        in_specs=in_specs,
        out_specs=VMEM,
        scratch_shapes=list(scratch),
        cost_estimate=pl.CostEstimate(flops=cost[0], bytes_accessed=cost[1], transcendentals=0),
        compiler_params=pltpu.CompilerParams(vmem_limit_bytes=48 << 20),
    )


def reversed_bits(value, count):
    result = 0
    while count > 1:
        result = result * 2 + value % 2
        value //= 2
        count //= 2
    return result


def lane_tiles(image_ref, stage, index):
    lines = image_ref.shape[-1]
    whole = lines // LANES
    tiles = [image_ref[index + (slice(None), slice(k * LANES, (k + 1) * LANES))] for k in range(whole)]
    stage[:, 0 : lines - whole * LANES] = image_ref[index + (slice(None), slice(whole * LANES, lines))]
    return tiles + [stage[...]]


def candidate_body(group, dates_ref, me_ref, x_ref, out_ref, stage):
    cols, lines = x_ref.shape[-2:]
    chips_az = (lines - 2 * MARGIN) // CHIP
    lane = lane_index((cols, LANES))
    octets = out_ref.shape[0] // 8 // group

    def place(octet):
        return (reversed_bits(octet // octets, group) * octets + octet % octets) * 8

    parts = [[tile.astype(F32) for tile in lane_tiles(x_ref, stage.at[p], (0, 0, p))] for p in range(2)]
    for a in range(chips_az):
        start = MARGIN + a * CHIP
        tile, offset = start // LANES, start % LANES
        halves = []
        for p in range(2):
            shift = (p * CHIP - offset) % LANES
            value = pltpu.roll(parts[p][tile], shift, 1)
            if offset + CHIP > LANES:
                value = jnp.where(lane < p * CHIP + LANES - offset, value, pltpu.roll(parts[p][tile + 1], shift, 1))
            halves.append(value)
        value = jnp.where(lane < CHIP, halves[0], halves[1])
        for k in range(cols // 8):
            at = place(a * (cols // 8) + k)
            out_ref[at : at + 8, :] = value[8 * k : 8 * k + 8].astype(BF16)
    for octet in range(chips_az * cols // 8, out_ref.shape[0] // 8):
        at = place(octet)
        out_ref[at : at + 8, :] = jnp.zeros((8, LANES), BF16)


def resample_body(date, shift_ref, frac_ref, table_ref, x_ref, left_ref, right_ref, out_ref, stage, window):
    t = pl.program_id(0)
    cols, lines = x_ref.shape[-2:]
    chips_az = (lines - 2 * MARGIN) // CHIP
    chips_rg = cols // CHIP
    depth = CHIP + 2 * EDGE

    def fill(source_ref, scratch, at):
        count = source_ref.shape[-2]
        lane = lane_index((count, LANES))
        for p in range(2):
            tiles = lane_tiles(source_ref, scratch.at[p], (0, 0, p))
            turned = [pltpu.roll(tile, CHIP, 1) for tile in tiles]
            for a in range(chips_az):
                tile = tiles[a // 2]
                if a % 2:
                    tile = jnp.where(lane < CHIP, turned[a // 2], turned[a // 2 + 1])
                window[a, p, at : at + count, :] = tile

    for p in range(2):
        stage[p, :, :] = jnp.zeros(stage.shape[1:], BF16)
    fill(left_ref, stage.at[:, 0:EDGE], 0)
    fill(x_ref, stage, EDGE)
    fill(right_ref, stage.at[:, 0:EDGE], EDGE + cols)
    half = lane_index((depth, LANES)) < CHIP

    def skewed(fraction, offset):
        return pltpu.roll(table_ref[fraction], offset, 1)

    def chip_column(r, carry):
        start = pl.multiple_of(r * CHIP, CHIP)
        for a in range(chips_az):
            azimuth = skewed(frac_ref[0, date, a, t, r], shift_ref[0, date, a, t, r] + 9)
            across = skewed(frac_ref[1, date, a, t, r], shift_ref[1, date, a, t, r] + 13)
            both = jnp.concatenate([azimuth, azimuth], axis=0)
            data = jnp.concatenate([window[a, p, pl.ds(start, depth), :] for p in range(2)], axis=0)
            partial = lax.dot_general(data, both, (((1,), (1,)), ((), ())), preferred_element_type=F32)
            partial = jnp.where(half, partial[:depth], partial[depth:]).astype(BF16)
            chip = jnp.dot(across[:, :depth], partial, preferred_element_type=F32)
            out_ref[0, pl.ds(pl.multiple_of(a * cols + start, CHIP), CHIP), :] = chip.astype(BF16)
        return carry

    lax.fori_loop(0, chips_rg, chip_column, 0, unroll=UNROLL)


def pair_body(pair, plain_ref, signed_ref, a_ref, b_ref, *rest):
    if pair == 1:
        before_ref, out_ref, product, looked = rest
    else:
        out_ref, product, looked = rest
    chips_az = plain_ref.shape[1] // LANES
    cols = a_ref.shape[1] // chips_az
    looks = cols // LOOK_RG
    for t in range(2):
        for a in range(chips_az):
            first = a_ref[t, a * cols : (a + 1) * cols, :].astype(F32)
            second = b_ref[t, a * cols : (a + 1) * cols, :].astype(F32)
            product[0] = first * second
            product[1] = pltpu.roll(first, CHIP, 1) * second
            product[2] = first * first
            product[3] = second * second
            for q in range(4):
                total = product[q, pl.ds(0, looks, stride=LOOK_RG), :]
                for k in range(1, LOOK_RG):
                    total = total + product[q, pl.ds(k, looks, stride=LOOK_RG), :]
                row = (q * 2 + t) * looks
                looked[row : row + looks, a * LANES : (a + 1) * LANES] = total

    value = looked[...]
    top = value.astype(BF16)
    low = (value - top.astype(F32)).astype(BF16)

    def line_sums(matrix_ref):
        dims = (((1,), (1,)), ((), ()))
        matrix = matrix_ref[...]
        return lax.dot_general(matrix, top, dims, preferred_element_type=F32) + lax.dot_general(
            matrix, low, dims, preferred_element_type=F32
        )

    plain = line_sums(plain_ref)
    signed = line_sums(signed_ref)
    lane = lane_index(plain.shape)
    real = lane < LANES // 4
    by_32, by_64, by_96 = (pltpu.roll(plain, k, 1) for k in (32, 64, 96))
    power_first = jnp.where(real, by_64, by_96)
    power_second = jnp.where(real, by_32, by_64)
    value = jnp.where(real, plain, signed) / jnp.sqrt((power_first + EPSILON) * (power_second + EPSILON))
    if pair == 1:
        value = jnp.where(lane < CHIP, before_ref[...], pltpu.roll(value, CHIP, 1))
    out_ref[...] = value


def correlate_body(other, me_ref, ref_ref, s0_ref, s1_ref, out_ref, sums):
    half_chips = ref_ref.shape[1] // CHIP
    chips = s0_ref.shape[1] // CHIP
    half = lax.rem(me_ref[0], 2)
    base = (1 - half if other else half) * half_chips
    lane = lane_index((8, LANES))
    sign = jnp.where(lane < CHIP, 1.0, -1.0)

    def fold(value):
        total = value[0:8]
        for k in range(1, CHIP // 8):
            total = total + value[8 * k : 8 * k + 8]
        return total

    for t in range(2):

        def one_chip(k, carry):
            row = pl.multiple_of(k * CHIP, CHIP)
            source = pl.multiple_of(jnp.minimum(base + k, chips - 1) * CHIP, CHIP)
            ref = ref_ref[t, pl.ds(row, CHIP), :].astype(F32)
            turned = pltpu.roll(ref, CHIP, 1)
            power = jnp.sum(fold(ref * ref), axis=0, keepdims=True)
            for d, s_ref in enumerate((s0_ref, s1_ref)):
                sec = s_ref[t, pl.ds(source, CHIP), :].astype(F32)
                at = (d * 2 + t) * 16 + k
                sums[0, pl.ds(at, 1), :] = jnp.sum(fold(ref * sec), axis=0, keepdims=True)
                sums[1, pl.ds(at, 1), :] = jnp.sum(fold(turned * sec) * sign, axis=0, keepdims=True)
                sums[2, pl.ds(at, 1), :] = jnp.sum(fold(sec * sec), axis=0, keepdims=True)
                sums[3, pl.ds(at, 1), :] = power
            return carry

        lax.fori_loop(0, half_chips, one_chip, 0)
        for d in range(2):
            at = (d * 2 + t) * 16 + half_chips
            sums[:, at : at + 16 - half_chips, :] = jnp.zeros((4, 16 - half_chips, LANES), F32)
    real, imag, sec_power, ref_power = (jnp.sum(sums[q], axis=1, keepdims=True) for q in range(4))
    denominator = jnp.sqrt((ref_power + EPSILON) * (sec_power + EPSILON))
    wide = lane_index(out_ref.shape)
    out_ref[...] = jnp.where(wide == 0, real, imag) / denominator


def per_device(acquisitions, shifts, fractions, ref_dates):
    dates, tiles, parts, rows, cols = acquisitions.shape
    group = lax.axis_size("date")
    strips = lax.axis_size("strip")
    me = lax.axis_index("date")
    me_one = me.reshape(1).astype(jnp.int32)
    chips_az = (rows - 2 * MARGIN) // CHIP
    chips_rg = cols // CHIP
    chips = chips_az * chips_rg
    lines = chips * CHIP
    looks = cols // LOOK_RG
    blocks = chips_az * CHIP // LOOK_AZ
    piece = -(-lines // (group * 8)) * 8
    shape = jax.ShapeDtypeStruct
    image_bytes = rows * cols * 2
    images = acquisitions.transpose(0, 1, 2, 4, 3)
    shifts = shifts.transpose(0, 1, 3, 2, 4)
    fractions = fractions.transpose(0, 1, 3, 2, 4)
    owners = ref_dates // dates

    table = jnp.asarray(tap_table())
    plain, signed = (jnp.asarray(m) for m in look_matrices(chips_az * CHIP))

    left = lax.ppermute(images[:, :, :, cols - EDGE :], "strip", [(i, i + 1) for i in range(strips - 1)])
    right = lax.ppermute(images[:, :, :, :EDGE], "strip", [(i + 1, i) for i in range(strips - 1)])

    def owned(step, dates_ref, me_ref):
        tile = (dates_ref[1] // dates == me_ref[0]).astype(jnp.int32)
        return (lax.rem(dates_ref[tile], dates), tile, 0, 0, 0)

    candidate = pl.pallas_call(
        functools.partial(candidate_body, group),
        out_shape=shape((piece * group, LANES), BF16),
        grid_spec=pltpu.PrefetchScalarGridSpec(
            num_scalar_prefetch=2,
            grid=(1,),
            in_specs=[pl.BlockSpec((1, 1, parts, cols, rows), owned)],
            out_specs=pl.BlockSpec((piece * group, LANES), lambda *_: (0, 0)),
            scratch_shapes=[pltpu.VMEM((parts, cols, LANES), BF16)],
        ),
        cost_estimate=pl.CostEstimate(flops=10**6, bytes_accessed=4 * image_bytes, transcendentals=0),
        compiler_params=pltpu.CompilerParams(vmem_limit_bytes=32 << 20),
    )(ref_dates, me_one, images)
    scattered = lax.all_to_all(candidate.reshape(group, piece, LANES), "date", 0, 0, tiled=True)
    reference = jnp.concatenate([lax.dynamic_slice_in_dim(scattered, owners[t], 1) for t in range(tiles)])

    def resample(d):
        def of_tile(t):
            return (d, t, 0, 0, 0)

        edge = pl.BlockSpec((1, 1, parts, EDGE, rows), of_tile)
        return pl.pallas_call(
            functools.partial(resample_body, d),
            out_shape=shape((tiles, lines, LANES), BF16),
            grid=(tiles,),
            in_specs=[
                SMEM,
                SMEM,
                pl.BlockSpec(table.shape, lambda t: (0, 0, 0), pipeline_mode=pl.Buffered(1)),
                pl.BlockSpec((1, 1, parts, cols, rows), of_tile),
                edge,
                edge,
            ],
            out_specs=pl.BlockSpec((1, lines, LANES), lambda t: (t, 0, 0)),
            scratch_shapes=[
                pltpu.VMEM((parts, cols, LANES), BF16),
                pltpu.VMEM((chips_az, parts, cols + 2 * EDGE, LANES), BF16),
            ],
            cost_estimate=pl.CostEstimate(
                flops=tiles * chips * 64 * 128 * 256 * 4, bytes_accessed=8 * image_bytes, transcendentals=0
            ),
            compiler_params=pltpu.CompilerParams(vmem_limit_bytes=32 << 20),
        )(shifts, fractions, table, images, left, right)

    def pair(index, *values):
        return call(
            functools.partial(pair_body, index),
            shape((blocks, LANES), F32),
            [VMEM] * (2 + len(values)),
            [
                pltpu.VMEM((4, cols, LANES), F32),
                pltpu.VMEM((4 * tiles * looks, chips_az * LANES), F32),
            ],
            cost=(10**8, 8 * image_bytes),
        )(plain, signed, *values)

    def correlate(other, value):
        return call(
            functools.partial(correlate_body, other),
            shape((4 * 16, LANES), F32),
            [SMEM, VMEM, VMEM, VMEM],
            [pltpu.VMEM((4, 4 * 16, LANES), F32)],
            cost=(10**7, 3 * image_bytes),
        )(me_one, value.reshape(tiles, -1, LANES), first, second)

    def exchange(value, step):
        other = lax.ppermute(value, "date", [(i, i ^ step) for i in range(group)])
        high = (me & step) != 0
        return jnp.concatenate([jnp.where(high, other, value), jnp.where(high, value, other)], axis=1)

    def after(value, *events):
        return lax.optimization_barrier((value,) + events)[0]

    first = resample(0)
    following = lax.ppermute(first, "date", [(i + 1, i) for i in range(group - 1)])
    reference = exchange(after(reference, first), 16)
    second = resample(1)
    reference = exchange(after(reference, second), 8)
    looked = pair(0, first, second)
    reference = exchange(after(reference, looked), 4)
    looked = pair(1, second, following, looked)
    reference = exchange(after(reference, looked), 2)
    relayed = lax.all_to_all(looked.reshape(group, -1, LANES), "date", 0, 0, tiled=True)
    other = lax.ppermute(reference, "date", [(i, i ^ 1) for i in range(group)])

    relayed = relayed.reshape(group, blocks // group, 2, 2, tiles, looks)
    coherence = relayed.transpose(3, 0, 2, 4, 1, 5).reshape(2, 2 * group, tiles, blocks // group, looks)
    coherence = coherence[:, : 2 * group - 1]

    here = correlate(False, reference)
    there = correlate(True, other)
    half = me & 1
    half_chips = piece * group // 2 // CHIP
    low = jnp.where(half == 0, here, there).reshape(4, 16, LANES)[:, :half_chips, :2]
    high = jnp.where(half == 0, there, here).reshape(4, 16, LANES)[:, : chips - half_chips, :2]
    chip_corr = jnp.concatenate([low, high], axis=1).reshape(dates, tiles, chips_az, chips_rg, 2)
    return chip_corr.transpose(4, 0, 1, 2, 3), coherence


def solution(mesh):
    return jax.shard_map(
        per_device,
        mesh=mesh,
        in_specs=(
            P("date", None, None, None, "strip"),
            P(None, "date", None, None, "strip"),
            P(None, "date", None, None, "strip"),
            P(),
        ),
        out_specs=(P(None, "date", None, None, "strip"), P(None, None, None, "date", "strip")),
        check_vma=False,
    )
```

```python
import functools

import jax
import jax.numpy as jnp
import numpy as np
from jax import lax
from jax.experimental import pallas as pl
from jax.experimental.pallas import tpu as pltpu
from jax.sharding import PartitionSpec as P

CHIP = 64
TAPS = 8
SUBSTEPS = 64
LOOK_AZ = 5
LOOK_RG = 20
MARGIN = 12
WINDOW = CHIP + 2 * MARGIN
LANES = 128
EDGE = 16
SKEW = 16
PACK = 16
EPSILON = 1e-06

VMEM = pl.BlockSpec(memory_space=pltpu.VMEM)
SMEM = pl.BlockSpec(memory_space=pltpu.SMEM)
F32 = jnp.float32
BF16 = jnp.bfloat16


def tap_table():
    x = np.arange(TAPS)[None, :] - (TAPS // 2 - 1) - np.arange(SUBSTEPS)[:, None] / SUBSTEPS
    weights = np.sinc(x) * (0.5 + 0.5 * np.cos(2 * np.pi * x / TAPS))
    weights = weights / weights.sum(axis=1, keepdims=True)
    table = np.zeros((SUBSTEPS, SKEW, LANES), np.float32)
    for line in range(SKEW):
        table[:, line, line : line + TAPS] = weights
    return table.astype(jnp.bfloat16)


def look_matrices(lines):
    chips = lines // CHIP
    looks = lines // LOOK_AZ
    plain = np.zeros((looks, chips, 2, CHIP), np.float32)
    for line in range(lines):
        plain[line // LOOK_AZ, line // CHIP, :, line % CHIP] = 1.0
    signed = plain.copy()
    signed[:, :, 1] *= -1.0
    return [m.reshape(looks, chips * LANES).astype(jnp.bfloat16) for m in (plain, signed)]


def lane_index(shape):
    return lax.broadcasted_iota(jnp.int32, shape, len(shape) - 1)


def call(body, outs, in_specs, scratch=(), cost=(0, 0)):
    return pl.pallas_call(
        body,
        out_shape=outs,
        in_specs=in_specs,
        out_specs=VMEM,
        scratch_shapes=list(scratch),
        cost_estimate=pl.CostEstimate(flops=cost[0], bytes_accessed=cost[1], transcendentals=0),
        compiler_params=pltpu.CompilerParams(vmem_limit_bytes=48 << 20),
    )


def reversed_bits(value, count):
    result = 0
    while count > 1:
        result = result * 2 + value % 2
        value //= 2
        count //= 2
    return result


def lane_tiles(image_ref, stage, index):
    lines = image_ref.shape[-1]
    whole = lines // LANES
    tiles = [image_ref[index + (slice(None), slice(k * LANES, (k + 1) * LANES))] for k in range(whole)]
    stage[:, 0 : lines - whole * LANES] = image_ref[index + (slice(None), slice(whole * LANES, lines))]
    return tiles + [stage[...]]


def candidate_body(group, dates_ref, me_ref, x_ref, out_ref, stage):
    cols, lines = x_ref.shape[-2:]
    chips_az = (lines - 2 * MARGIN) // CHIP
    lane = lane_index((cols, LANES))
    steps = out_ref.shape[0] // PACK // group

    def place(step):
        return (reversed_bits(step // steps, group) * steps + step % steps) * PACK

    parts = [lane_tiles(x_ref, stage.at[p], (0, 0, p)) for p in range(2)]
    for a in range(chips_az):
        start = MARGIN + a * CHIP
        tile, offset = start // LANES, start % LANES
        halves = []
        for p in range(2):
            shift = (p * CHIP - offset) % LANES
            value = pltpu.roll(parts[p][tile], shift, 1)
            if offset + CHIP > LANES:
                value = jnp.where(lane < p * CHIP + LANES - offset, value, pltpu.roll(parts[p][tile + 1], shift, 1))
            halves.append(value)
        value = jnp.where(lane < CHIP, halves[0], halves[1])
        for k in range(cols // PACK):
            at = place(a * (cols // PACK) + k)
            out_ref[at : at + PACK, :] = value[PACK * k : PACK * (k + 1)]
    for step in range(chips_az * cols // PACK, out_ref.shape[0] // PACK):
        at = place(step)
        out_ref[at : at + PACK, :] = jnp.zeros((PACK, LANES), BF16)


def resample_body(date, shift_ref, frac_ref, table_ref, x_ref, left_ref, right_ref, out_ref, stage, window):
    t = pl.program_id(0)
    cols, lines = x_ref.shape[-2:]
    chips_az = (lines - 2 * MARGIN) // CHIP
    chips_rg = cols // CHIP
    depth = CHIP + 2 * EDGE

    def fill(source_ref, scratch, at):
        count = source_ref.shape[-2]
        lane = lane_index((count, LANES))
        for p in range(2):
            tiles = lane_tiles(source_ref, scratch.at[p], (0, 0, p))
            turned = [pltpu.roll(tile, CHIP, 1) for tile in tiles]
            for a in range(chips_az):
                tile = tiles[a // 2]
                if a % 2:
                    tile = jnp.where(lane < CHIP, turned[a // 2], turned[a // 2 + 1])
                window[a, p, at : at + count, :] = tile

    for p in range(2):
        stage[p, :, :] = jnp.zeros(stage.shape[1:], BF16)
    fill(left_ref, stage.at[:, 0:EDGE], 0)
    fill(x_ref, stage, EDGE)
    fill(right_ref, stage.at[:, 0:EDGE], EDGE + cols)
    half = lane_index((depth, LANES)) < CHIP

    def skewed(fraction, offset):
        base = table_ref[fraction]
        return jnp.concatenate([pltpu.roll(base, offset + k, 1) for k in range(0, CHIP, SKEW)], axis=0)

    for r in range(chips_rg):
        start = r * CHIP
        firsts = []
        for a in range(chips_az):
            azimuth = skewed(frac_ref[0, date, a, t, r], shift_ref[0, date, a, t, r] + 9)
            both = jnp.concatenate([azimuth, azimuth], axis=0)
            data = jnp.concatenate([window[a, p, start : start + depth, :] for p in range(2)], axis=0)
            partial = lax.dot_general(data, both, (((1,), (1,)), ((), ())), preferred_element_type=F32)
            firsts.append(jnp.where(half, partial[:depth], partial[depth:]).astype(BF16))
        if r:
            for a in range(chips_az):
                across = skewed(frac_ref[1, date, a, t, r - 1], shift_ref[1, date, a, t, r - 1] + 13)
                chip = jnp.dot(across[:, :depth], before[a], preferred_element_type=F32)
                out_ref[0, a * cols + start - CHIP : a * cols + start, :] = chip.astype(BF16)
        before = firsts
    for a in range(chips_az):
        across = skewed(frac_ref[1, date, a, t, r], shift_ref[1, date, a, t, r] + 13)
        chip = jnp.dot(across[:, :depth], before[a], preferred_element_type=F32)
        out_ref[0, a * cols + start : a * cols + start + CHIP, :] = chip.astype(BF16)


def resample_call(d, shifts, fractions, table, images, left, right):
    dates, tiles, parts, cols, rows = images.shape
    chips_az = (rows - 2 * MARGIN) // CHIP
    lines = chips_az * cols

    def of_tile(t):
        return (d, t, 0, 0, 0)

    edge = pl.BlockSpec((1, 1, parts, EDGE, rows), of_tile)
    return pl.pallas_call(
        functools.partial(resample_body, d),
        out_shape=jax.ShapeDtypeStruct((tiles, lines, LANES), BF16),
        grid=(tiles,),
        in_specs=[
            SMEM,
            SMEM,
            pl.BlockSpec(table.shape, lambda t: (0, 0, 0)),
            pl.BlockSpec((1, 1, parts, cols, rows), of_tile),
            edge,
            edge,
        ],
        out_specs=pl.BlockSpec((1, lines, LANES), lambda t: (t, 0, 0)),
        scratch_shapes=[
            pltpu.VMEM((parts, cols, LANES), BF16),
            pltpu.VMEM((chips_az, parts, cols + 2 * EDGE, LANES), BF16),
        ],
        cost_estimate=pl.CostEstimate(
            flops=tiles * lines * 128 * 256 * 4, bytes_accessed=16 * rows * cols, transcendentals=0
        ),
        compiler_params=pltpu.CompilerParams(vmem_limit_bytes=60 << 20),
    )(shifts, fractions, table, images, left, right)


def pair_body(pair, plain_ref, signed_ref, a_ref, b_ref, *rest):
    if pair == 1:
        before_ref, out_ref, product, looked = rest
    else:
        out_ref, product, looked = rest
    chips_az = plain_ref.shape[1] // LANES
    cols = a_ref.shape[1] // chips_az
    looks = cols // LOOK_RG
    for t in range(2):
        for a in range(chips_az):
            first = a_ref[t, a * cols : (a + 1) * cols, :].astype(F32)
            second = b_ref[t, a * cols : (a + 1) * cols, :].astype(F32)
            work = product.at[a % 2]
            work[0] = first * second
            work[1] = pltpu.roll(first, CHIP, 1) * second
            work[2] = first * first
            work[3] = second * second
            for q in range(4):
                total = work[q, pl.ds(0, looks, stride=LOOK_RG), :]
                for k in range(1, LOOK_RG):
                    total = total + work[q, pl.ds(k, looks, stride=LOOK_RG), :]
                row = (q * 2 + t) * looks
                looked[row : row + looks, a * LANES : (a + 1) * LANES] = total

    value = looked[...]
    top = value.astype(BF16)
    low = (value - top.astype(F32)).astype(BF16)

    def line_sums(matrix_ref):
        dims = (((1,), (1,)), ((), ()))
        matrix = matrix_ref[...]
        return lax.dot_general(matrix, top, dims, preferred_element_type=F32) + lax.dot_general(
            matrix, low, dims, preferred_element_type=F32
        )

    plain = line_sums(plain_ref)
    signed = line_sums(signed_ref)
    lane = lane_index(plain.shape)
    real = lane < LANES // 4
    by_32, by_64, by_96 = (pltpu.roll(plain, k, 1) for k in (32, 64, 96))
    power_first = jnp.where(real, by_64, by_96)
    power_second = jnp.where(real, by_32, by_64)
    value = jnp.where(real, plain, signed) / jnp.sqrt((power_first + EPSILON) * (power_second + EPSILON))
    if pair == 1:
        value = jnp.where(lane < CHIP, before_ref[...], pltpu.roll(value, CHIP, 1))
    out_ref[...] = value


def correlate_body(other, me_ref, ref_ref, s0_ref, s1_ref, out_ref, sums):
    half_chips = ref_ref.shape[1] // CHIP
    chips = s0_ref.shape[1] // CHIP
    half = lax.rem(me_ref[0], 2)
    base = (1 - half if other else half) * half_chips
    lane = lane_index((8, LANES))
    sign = jnp.where(lane < CHIP, 1.0, -1.0)

    def fold(value):
        total = value[0:8]
        for k in range(1, CHIP // 8):
            total = total + value[8 * k : 8 * k + 8]
        return total

    def total(value):
        return jnp.sum(fold(value), axis=0, keepdims=True)

    for t in range(2):
        for k in range(half_chips):
            source = pl.multiple_of(jnp.minimum(base + k, chips - 1) * CHIP, CHIP)
            ref = ref_ref[t, k * CHIP : (k + 1) * CHIP, :].astype(F32)
            turned = pltpu.roll(ref, CHIP, 1)
            power = total(ref * ref)
            for d, s_ref in enumerate((s0_ref, s1_ref)):
                sec = s_ref[t, pl.ds(source, CHIP), :].astype(F32)
                at = (d * 2 + t) * 16 + k
                sums[0, at : at + 1, :] = total(ref * sec)
                sums[1, at : at + 1, :] = jnp.sum(fold(turned * sec) * sign, axis=0, keepdims=True)
                sums[2, at : at + 1, :] = total(sec * sec)
                sums[3, at : at + 1, :] = power
        for d in range(2):
            at = (d * 2 + t) * 16 + half_chips
            sums[:, at : at + 16 - half_chips, :] = jnp.zeros((4, 16 - half_chips, LANES), F32)
    real, imag, sec_power, ref_power = (jnp.sum(sums[q], axis=1, keepdims=True) for q in range(4))
    denominator = jnp.sqrt((ref_power + EPSILON) * (sec_power + EPSILON))
    wide = lane_index(out_ref.shape)
    out_ref[...] = jnp.where(wide == 0, real, imag) / denominator


def per_device(acquisitions, shifts, fractions, ref_dates):
    dates, tiles, parts, rows, cols = acquisitions.shape
    group = lax.axis_size("date")
    strips = lax.axis_size("strip")
    me = lax.axis_index("date")
    me_one = me.reshape(1).astype(jnp.int32)
    chips_az = (rows - 2 * MARGIN) // CHIP
    chips_rg = cols // CHIP
    chips = chips_az * chips_rg
    lines = chips * CHIP
    looks = cols // LOOK_RG
    blocks = chips_az * CHIP // LOOK_AZ
    near = 8
    piece = -(-lines // (near * 2 * PACK)) * 2 * PACK
    shape = jax.ShapeDtypeStruct
    image_bytes = rows * cols * 2
    images = acquisitions.transpose(0, 1, 2, 4, 3)
    shifts = shifts.transpose(0, 1, 3, 2, 4)
    fractions = fractions.transpose(0, 1, 3, 2, 4)
    owners = ref_dates // dates

    table = jnp.asarray(tap_table())
    plain, signed = (jnp.asarray(m) for m in look_matrices(chips_az * CHIP))

    high_edge = images[:, :, :, cols - EDGE :]
    low_edge = images[:, :, :, :EDGE]
    left = lax.ppermute(high_edge, "strip", [(i, i + 1) for i in range(strips - 1)])
    right = lax.ppermute(low_edge, "strip", [(i + 1, i) for i in range(strips - 1)])

    def after(value, *events):
        return lax.optimization_barrier((value, events))[0]

    def owned(step, dates_ref, me_ref):
        tile = (dates_ref[1] // dates == me_ref[0]).astype(jnp.int32)
        return (lax.rem(dates_ref[tile], dates), tile, 0, 0, 0)

    candidate = pl.pallas_call(
        functools.partial(candidate_body, near),
        out_shape=shape((piece * near, LANES), BF16),
        grid_spec=pltpu.PrefetchScalarGridSpec(
            num_scalar_prefetch=2,
            grid=(1,),
            in_specs=[pl.BlockSpec((1, 1, parts, cols, rows), owned)],
            out_specs=pl.BlockSpec((piece * near, LANES), lambda *_: (0, 0)),
            scratch_shapes=[pltpu.VMEM((parts, cols, LANES), BF16)],
        ),
        cost_estimate=pl.CostEstimate(flops=10**6, bytes_accessed=4 * image_bytes, transcendentals=0),
        compiler_params=pltpu.CompilerParams(vmem_limit_bytes=60 << 20),
    )(after(ref_dates, high_edge, low_edge), me_one, images)
    scattered = lax.all_to_all(
        candidate.reshape(near, piece, LANES),
        "date",
        0,
        0,
        axis_index_groups=[list(range(k, k + near)) for k in range(0, group, near)],
        tiled=True,
    )
    from_owner = jnp.arange(near)[None, :] == (owners % near)[:, None]
    reference = jnp.sum(jnp.where(from_owner[:, :, None, None], scattered[None], 0), axis=1, dtype=BF16)
    left, right = after((left, right), reference)

    resample = functools.partial(resample_call, shifts=shifts, fractions=fractions, table=table, images=images, left=left, right=right)

    def pair(index, *values):
        return call(
            functools.partial(pair_body, index),
            shape((blocks, LANES), F32),
            [VMEM] * (2 + len(values)),
            [
                pltpu.VMEM((2, 4, cols, LANES), F32),
                pltpu.VMEM((4 * tiles * looks, chips_az * LANES), F32),
            ],
            cost=(10**8, 8 * image_bytes),
        )(plain, signed, *values)

    def correlate(other, value):
        return call(
            functools.partial(correlate_body, other),
            shape((4 * 16, LANES), F32),
            [SMEM, VMEM, VMEM, VMEM],
            [pltpu.VMEM((4, 4 * 16, LANES), F32)],
            cost=(10**7, 3 * image_bytes),
        )(me_one, value.reshape(tiles, -1, LANES), first, second)

    def exchange(value, step):
        other = lax.ppermute(value, "date", [(i, i ^ step) for i in range(group)])
        high = (me & step) != 0
        return jnp.concatenate([jnp.where(high, other, value), jnp.where(high, value, other)], axis=1)

    def flood(value, step):
        other = lax.ppermute(value, "date", [(i, i ^ step) for i in range(group)])
        same = ((me ^ owners) & step) == 0
        return jnp.where(same[:, None, None], value, other)

    reference = flood(reference, 16)
    first = resample(0)
    following = lax.ppermute(first, "date", [(i + 1, i) for i in range(group - 1)])
    reference = flood(after(reference, first), 8)
    second = resample(1)
    looked = pair(0, first, second)
    reference = exchange(after(reference, looked), 4)
    looked = pair(1, second, following, looked)
    relayed = lax.all_to_all(looked.reshape(group, -1, LANES), "date", 0, 0, tiled=True)
    reference = exchange(after(reference, looked), 2)
    reference, relayed = lax.optimization_barrier((reference, relayed))
    other = lax.ppermute(reference, "date", [(i, i ^ 1) for i in range(group)])

    relayed = relayed.reshape(group, blocks // group, 2, 2, tiles, looks)
    coherence = relayed.transpose(3, 0, 2, 4, 1, 5).reshape(2, 2 * group, tiles, blocks // group, looks)
    coherence = coherence[:, : 2 * group - 1]

    here = correlate(False, reference)
    there = correlate(True, other)
    half = me & 1
    half_chips = piece * near // 2 // CHIP
    low = jnp.where(half == 0, here, there).reshape(4, 16, LANES)[:, :half_chips, :2]
    high = jnp.where(half == 0, there, here).reshape(4, 16, LANES)[:, : chips - half_chips, :2]
    chip_corr = jnp.concatenate([low, high], axis=1).reshape(dates, tiles, chips_az, chips_rg, 2)
    return chip_corr.transpose(4, 0, 1, 2, 3), coherence


def solution(mesh):
    return jax.shard_map(
        per_device,
        mesh=mesh,
        in_specs=(
            P("date", None, None, None, "strip"),
            P(None, "date", None, None, "strip"),
            P(None, "date", None, None, "strip"),
            P(),
        ),
        out_specs=(P(None, "date", None, None, "strip"), P(None, None, None, "date", "strip")),
        check_vma=False,
    )
```

```python
import functools

import jax
import jax.numpy as jnp
import numpy as np
from jax import lax
from jax.experimental import pallas as pl
from jax.experimental.pallas import tpu as pltpu
from jax.sharding import PartitionSpec as P

CHIP = 64
TAPS = 8
SUBSTEPS = 64
MAX_SHIFT = 8
LOOK_AZ = 5
LOOK_RG = 20
MARGIN = 12
WINDOW = CHIP + 2 * MARGIN
LANES = 128
EDGE = 16
SKEW = 16
PACK = 16
EPSILON = 1e-06

VMEM = pl.BlockSpec(memory_space=pltpu.VMEM)
SMEM = pl.BlockSpec(memory_space=pltpu.SMEM)
F32 = jnp.float32
BF16 = jnp.bfloat16


def tap_table():
    x = np.arange(TAPS)[None, :] - (TAPS // 2 - 1) - np.arange(SUBSTEPS)[:, None] / SUBSTEPS
    weights = np.sinc(x) * (0.5 + 0.5 * np.cos(2 * np.pi * x / TAPS))
    weights = weights / weights.sum(axis=1, keepdims=True)
    table = np.zeros((SUBSTEPS, SKEW, LANES), np.float32)
    for line in range(SKEW):
        table[:, line, line : line + TAPS] = weights
    return table.astype(jnp.bfloat16)


def look_matrices(lines):
    chips = lines // CHIP
    looks = lines // LOOK_AZ
    plain = np.zeros((looks, chips, 2, CHIP), np.float32)
    for line in range(lines):
        plain[line // LOOK_AZ, line // CHIP, :, line % CHIP] = 1.0
    signed = plain.copy()
    signed[:, :, 1] *= -1.0
    return [m.reshape(looks, chips * LANES).astype(jnp.bfloat16) for m in (plain, signed)]


def lane_index(shape):
    return lax.broadcasted_iota(jnp.int32, shape, len(shape) - 1)


def call(body, outs, in_specs, scratch=(), cost=(0, 0)):
    return pl.pallas_call(
        body,
        out_shape=outs,
        in_specs=in_specs,
        out_specs=VMEM,
        scratch_shapes=list(scratch),
        cost_estimate=pl.CostEstimate(flops=cost[0], bytes_accessed=cost[1], transcendentals=0),
        compiler_params=pltpu.CompilerParams(vmem_limit_bytes=24 << 20),
    )


def reversed_bits(value, count):
    result = 0
    while count > 1:
        result = result * 2 + value % 2
        value //= 2
        count //= 2
    return result


def lane_tiles(read, lines, stage):
    whole = lines // LANES
    stage[:, 0 : lines - whole * LANES] = read(slice(whole * LANES, lines))
    return [read(slice(k * LANES, (k + 1) * LANES)) for k in range(whole)] + [stage[...]]


def candidate_body(group, dates_ref, me_ref, x_ref, out_ref, stage):
    cols, lines = x_ref.shape[-2:]
    chips_az = (lines - 2 * MARGIN) // CHIP
    lane = lane_index((cols, LANES))
    steps = out_ref.shape[0] // PACK // group

    def place(step):
        return (reversed_bits(step // steps, group) * steps + step % steps) * PACK

    parts = [lane_tiles(lambda part, p=p: x_ref[0, 0, p, :, part], lines, stage.at[p]) for p in range(2)]
    for a in range(chips_az):
        start = MARGIN + a * CHIP
        tile, offset = start // LANES, start % LANES
        halves = []
        for p in range(2):
            shift = (p * CHIP - offset) % LANES
            value = pltpu.roll(parts[p][tile], shift, 1)
            if offset + CHIP > LANES:
                value = jnp.where(lane < p * CHIP + LANES - offset, value, pltpu.roll(parts[p][tile + 1], shift, 1))
            halves.append(value)
        value = jnp.where(lane < CHIP, halves[0], halves[1])
        for k in range(cols // PACK):
            at = place(a * (cols // PACK) + k)
            out_ref[at : at + PACK, :] = value[PACK * k : PACK * (k + 1)]
    for step in range(chips_az * cols // PACK, out_ref.shape[0] // PACK):
        at = place(step)
        out_ref[at : at + PACK, :] = jnp.zeros((PACK, LANES), BF16)


def resample_body(crossed, me_ref, move_ref, table_ref, x_ref, left_ref, right_ref, *rest):
    out_refs = rest[: 2 if crossed else 4]
    stage, window, chips_ref = rest[len(out_refs) :]
    date = pl.program_id(0)
    t = 1 - date if crossed else date
    cols, lines = x_ref.shape[-2:]
    chips_az = (lines - 2 * MARGIN) // CHIP
    chips_rg = cols // CHIP
    depth = CHIP + 2 * EDGE

    def fill(read, count, scratch, at):
        lane = lane_index((count, LANES))
        for p in range(2):
            tiles = lane_tiles(functools.partial(read, p), lines, scratch.at[p])
            turned = [pltpu.roll(tile, CHIP, 1) for tile in tiles]
            for a in range(chips_az):
                tile = tiles[a // 2]
                if a % 2:
                    tile = jnp.where(lane < CHIP, turned[a // 2], turned[a // 2 + 1])
                window[a, p, at : at + count, :] = tile

    def left(p, part):
        return left_ref[0, 0, p, :, part]

    def right(p, part):
        return right_ref[0, 0, p, :, part]

    for p in range(2):
        stage[p, :, :] = jnp.zeros(stage.shape[1:], BF16)
    fill(left, EDGE, stage.at[:, 0:EDGE], 0)
    fill(lambda p, part: x_ref[0, 0, p, :, part], cols, stage, EDGE)
    fill(right, EDGE, stage.at[:, 0:EDGE], EDGE + cols)
    half = lane_index((depth, LANES)) < CHIP

    def skewed(move, offset):
        offset = offset - MAX_SHIFT + lax.div(move, SUBSTEPS)
        base = table_ref[lax.rem(move, SUBSTEPS)]
        return jnp.concatenate([pltpu.roll(base, offset + k, 1) for k in range(0, CHIP, SKEW)], axis=0)

    for r in range(chips_rg):
        start = r * CHIP
        firsts = []
        for a in range(chips_az):
            azimuth = skewed(move_ref[0, date, a, t, r], 9)
            both = jnp.concatenate([azimuth, azimuth], axis=0)
            data = jnp.concatenate([window[a, p, start : start + depth, :] for p in range(2)], axis=0)
            partial = lax.dot_general(data, both, (((1,), (1,)), ((), ())), preferred_element_type=F32)
            firsts.append(jnp.where(half, partial[:depth], partial[depth:]).astype(BF16))
        if r:
            for a in range(chips_az):
                across = skewed(move_ref[1, date, a, t, r - 1], 13)
                chip = jnp.dot(across[:, :depth], before[a], preferred_element_type=F32)
                chips_ref[a * cols + start - CHIP : a * cols + start, :] = chip.astype(BF16)
        before = firsts
    for a in range(chips_az):
        across = skewed(move_ref[1, date, a, t, r], 13)
        chip = jnp.dot(across[:, :depth], before[a], preferred_element_type=F32)
        chips_ref[a * cols + start : a * cols + start + CHIP, :] = chip.astype(BF16)

    for d in range(2):

        @pl.when(date == d)
        def _(d=d):
            out_refs[d][...] = chips_ref[...]

    if not crossed:
        parity = lax.rem(me_ref[0], 2)
        for side in range(2):

            @pl.when((date + parity + side) % 2 == 1)
            def _(side=side):
                out_refs[2 + side][...] = chips_ref[...]


def resample_call(crossed, me, moves, table, images, edges):
    dates, tiles, parts, cols, rows = images.shape
    chips_az = (rows - 2 * MARGIN) // CHIP
    lines = chips_az * cols

    count = 2 if crossed else 4

    def of_tile(date):
        return (date, 1 - date if crossed else date, 0, 0, 0)

    edge = pl.BlockSpec((1, 1, parts, EDGE, rows), of_tile)
    return pl.pallas_call(
        functools.partial(resample_body, crossed),
        out_shape=[jax.ShapeDtypeStruct((lines, LANES), BF16)] * count,
        grid=(dates,),
        in_specs=[
            SMEM,
            SMEM,
            pl.BlockSpec(table.shape, lambda date: (0, 0, 0)),
            pl.BlockSpec((1, 1, parts, cols, rows), of_tile),
            edge,
            edge,
        ],
        out_specs=[pl.BlockSpec((lines, LANES), lambda date: (0, 0))] * count,
        scratch_shapes=[
            pltpu.VMEM((parts, cols, LANES), BF16),
            pltpu.VMEM((chips_az, parts, cols + 2 * EDGE, LANES), BF16),
            pltpu.VMEM((lines, LANES), BF16),
        ],
        cost_estimate=pl.CostEstimate(
            flops=tiles * lines * 128 * 256 * 4, bytes_accessed=16 * rows * cols, transcendentals=0
        ),
        compiler_params=pltpu.CompilerParams(vmem_limit_bytes=16 << 20),
    )(me, moves, table, images, *edges)


def pair_body(pair, plain_ref, signed_ref, *rest):
    if pair == 1:
        me_ref, first_0, got1, got2, second_1, before_ref, out_ref, product, looked = rest
        even = lax.rem(me_ref[0], 2) == 0
        sources = [
            (lambda rows: first_0[rows, :], lambda rows: jnp.where(even, got1[rows, :], got2[rows, :])),
            (lambda rows: jnp.where(even, got2[rows, :], got1[rows, :]), lambda rows: second_1[rows, :]),
        ]
    else:
        first_0, second_0, first_1, second_1, out_ref, product, looked = rest
        sources = [
            (lambda rows: first_0[rows, :], lambda rows: second_0[rows, :]),
            (lambda rows: first_1[rows, :], lambda rows: second_1[rows, :]),
        ]
    chips_az = plain_ref.shape[1] // LANES
    cols = first_0.shape[0] // chips_az
    looks = cols // LOOK_RG
    for t, (read_first, read_second) in enumerate(sources):
        for a in range(chips_az):
            first = read_first(slice(a * cols, (a + 1) * cols)).astype(F32)
            second = read_second(slice(a * cols, (a + 1) * cols)).astype(F32)
            work = product.at[a % 2]
            work[0] = first * second
            work[1] = pltpu.roll(first, CHIP, 1) * second
            work[2] = first * first
            work[3] = second * second
            for q in range(4):
                total = work[q, pl.ds(0, looks, stride=LOOK_RG), :]
                for k in range(1, LOOK_RG):
                    total = total + work[q, pl.ds(k, looks, stride=LOOK_RG), :]
                row = (q * 2 + t) * looks
                looked[row : row + looks, a * LANES : (a + 1) * LANES] = total

    value = looked[...]
    top = value.astype(BF16)
    low = (value - top.astype(F32)).astype(BF16)

    def line_sums(matrix_ref):
        dims = (((1,), (1,)), ((), ()))
        matrix = matrix_ref[...]
        return lax.dot_general(matrix, top, dims, preferred_element_type=F32) + lax.dot_general(
            matrix, low, dims, preferred_element_type=F32
        )

    plain = line_sums(plain_ref)
    signed = line_sums(signed_ref)
    lane = lane_index(plain.shape)
    real = lane < LANES // 4
    by_32, by_64, by_96 = (pltpu.roll(plain, k, 1) for k in (32, 64, 96))
    power_first = jnp.where(real, by_64, by_96)
    power_second = jnp.where(real, by_32, by_64)
    value = jnp.where(real, plain, signed) / jnp.sqrt((power_first + EPSILON) * (power_second + EPSILON))
    if pair == 1:
        value = jnp.where(lane < CHIP, before_ref[...], pltpu.roll(value, CHIP, 1))
    out_ref[...] = value


def pair_places(group, blocks):
    places = np.zeros((group, blocks, blocks, 3, LANES), np.float32)
    for device in range(group):
        for block in range(blocks):
            for kind, p in enumerate((2 * device, 2 * device + 1, 2 * device - 1)):
                if 0 <= p < 2 * group - 1:
                    places[device, block, block, kind, p] = 1.0
    return places.reshape(group * blocks, blocks * 3 * LANES)


def assemble_body(places_ref, looked_ref, out_ref):
    pairs = out_ref.shape[-1]
    looks = out_ref.shape[-2]
    rows = jnp.transpose(looked_ref[...])
    spread = jnp.dot(rows, places_ref[...], precision=lax.Precision.HIGHEST, preferred_element_type=F32)
    for q in range(2):
        for t in range(2):
            low = (q * 2 + t) * looks
            for b in range(out_ref.shape[2]):
                at = b * 3 * LANES
                inner = spread[low : low + looks, at : at + LANES]
                at += (1 + t) * LANES
                outer = spread[CHIP + low : CHIP + low + looks, at : at + LANES]
                out_ref[q, t, b] = (inner + outer)[:, :pairs]


def correlate_body(other, me_ref, ref_ref, s00_ref, s01_ref, s10_ref, s11_ref, out_ref, sums):
    half_chips = ref_ref.shape[1] // CHIP
    chips = s00_ref.shape[0] // CHIP
    half = lax.rem(me_ref[0], 2)
    base = (1 - half if other else half) * half_chips
    lane = lane_index((8, LANES))
    sign = jnp.where(lane < CHIP, 1.0, -1.0)

    def fold(value):
        total = value[0:8]
        for k in range(1, CHIP // 8):
            total = total + value[8 * k : 8 * k + 8]
        return total

    def total(value):
        return jnp.sum(fold(value), axis=0, keepdims=True)

    for t in range(2):
        for k in range(half_chips):
            source = pl.multiple_of(jnp.minimum(base + k, chips - 1) * CHIP, CHIP)
            ref = ref_ref[t, k * CHIP : (k + 1) * CHIP, :].astype(F32)
            turned = pltpu.roll(ref, CHIP, 1)
            power = total(ref * ref)
            for d in range(2):
                s_ref = ((s00_ref, s01_ref), (s10_ref, s11_ref))[d][t]
                sec = s_ref[pl.ds(source, CHIP), :].astype(F32)
                at = (d * 2 + t) * 16 + k
                sums[0, at : at + 1, :] = total(ref * sec)
                sums[1, at : at + 1, :] = jnp.sum(fold(turned * sec) * sign, axis=0, keepdims=True)
                sums[2, at : at + 1, :] = total(sec * sec)
                sums[3, at : at + 1, :] = power
        for d in range(2):
            at = (d * 2 + t) * 16 + half_chips
            sums[:, at : at + 16 - half_chips, :] = jnp.zeros((4, 16 - half_chips, LANES), F32)
    real, imag, sec_power, ref_power = (jnp.sum(sums[q], axis=1, keepdims=True) for q in range(4))
    denominator = jnp.sqrt((ref_power + EPSILON) * (sec_power + EPSILON))
    wide = lane_index(out_ref.shape)
    out_ref[...] = jnp.where(wide == 0, real, imag) / denominator


def per_device(acquisitions, shifts, fractions, ref_dates):
    dates, tiles, parts, rows, cols = acquisitions.shape
    group = lax.axis_size("date")
    strips = lax.axis_size("strip")
    me = lax.axis_index("date")
    strip = lax.axis_index("strip")
    me_one = me.reshape(1).astype(jnp.int32)
    chips_az = (rows - 2 * MARGIN) // CHIP
    chips_rg = cols // CHIP
    chips = chips_az * chips_rg
    lines = chips * CHIP
    looks = cols // LOOK_RG
    blocks = chips_az * CHIP // LOOK_AZ
    near = 8
    piece = -(-lines // (near * 2 * PACK)) * 2 * PACK
    shape = jax.ShapeDtypeStruct
    image_bytes = rows * cols * 2
    images = acquisitions.transpose(0, 1, 2, 4, 3)
    moves = ((shifts + MAX_SHIFT) * SUBSTEPS + fractions).transpose(0, 1, 3, 2, 4)
    owners = ref_dates // dates

    table = jnp.asarray(tap_table())
    plain, signed = (jnp.asarray(m) for m in look_matrices(chips_az * CHIP))

    high_edge = images[:, :, :, cols - EDGE :]
    low_edge = images[:, :, :, :EDGE]
    even = strip % 2 == 0
    pairs1 = [(i, i ^ 1) for i in range(strips)]
    pairs2 = [(i, (i + 1 ^ 1) - 1) for i in range(1, strips - 1)]
    to_one, to_other = jnp.where(even, high_edge, low_edge), jnp.where(even, low_edge, high_edge)
    from_one = lax.ppermute(to_one, "strip", pairs1)
    from_other = lax.ppermute(to_other, "strip", pairs2)

    def after(value, *events):
        return lax.optimization_barrier((value, events))[0]

    def owned(step, dates_ref, me_ref):
        tile = (dates_ref[1] // dates == me_ref[0]).astype(jnp.int32)
        return (lax.rem(dates_ref[tile], dates), tile, 0, 0, 0)

    candidate = pl.pallas_call(
        functools.partial(candidate_body, near),
        out_shape=shape((piece * near, LANES), BF16),
        grid_spec=pltpu.PrefetchScalarGridSpec(
            num_scalar_prefetch=2,
            grid=(1,),
            in_specs=[pl.BlockSpec((1, 1, parts, cols, rows), owned)],
            out_specs=pl.BlockSpec((piece * near, LANES), lambda *_: (0, 0)),
            scratch_shapes=[pltpu.VMEM((parts, cols, LANES), BF16)],
        ),
        cost_estimate=pl.CostEstimate(flops=10**6, bytes_accessed=4 * image_bytes, transcendentals=0),
        compiler_params=pltpu.CompilerParams(vmem_limit_bytes=60 << 20),
    )(after(ref_dates, to_one, to_other), me_one, images)
    scattered = lax.all_to_all(
        candidate.reshape(near, piece, LANES),
        "date",
        0,
        0,
        axis_index_groups=[list(range(k, k + near)) for k in range(0, group, near)],
        tiled=True,
    )
    from_owner = jnp.arange(near)[None, :] == (owners % near)[:, None]
    reference = jnp.sum(jnp.where(from_owner[:, :, None, None], scattered[None], 0), axis=1, dtype=BF16)
    edges = (jnp.where(even, from_other, from_one), jnp.where(even, from_one, from_other))

    resample = functools.partial(resample_call, me=me_one, moves=moves, table=table, images=images, edges=edges)

    def pair(index, *values):
        return call(
            functools.partial(pair_body, index),
            shape((blocks, LANES), F32),
            [VMEM] * 2 + [SMEM] * index + [VMEM] * (len(values) - index),
            [
                pltpu.VMEM((2, 4, cols, LANES), F32),
                pltpu.VMEM((4 * tiles * looks, chips_az * LANES), F32),
            ],
            cost=(10**8, 8 * image_bytes),
        )(plain, signed, *values)

    def correlate(other, value):
        return call(
            functools.partial(correlate_body, other),
            shape((4 * 16, LANES), F32),
            [SMEM] + [VMEM] * 5,
            [pltpu.VMEM((4, 4 * 16, LANES), F32)],
            cost=(10**7, 3 * image_bytes),
        )(me_one, value.reshape(tiles, -1, LANES), s00, s01, s10, s11)

    def exchange(value, step):
        other = lax.ppermute(value, "date", [(i, i ^ step) for i in range(group)])
        high = (me & step) != 0
        return jnp.concatenate([jnp.where(high, other, value), jnp.where(high, value, other)], axis=1)

    def flood(value, step):
        other = lax.ppermute(value, "date", [(i, i ^ step) for i in range(group)])
        same = ((me ^ owners) & step) == 0
        return jnp.where(same[:, None, None], value, other)

    reference = flood(reference, 16)
    s00, s11, send1, send2 = resample(False)
    got1 = lax.ppermute(send1, "date", [(i, i ^ 1) for i in range(group)])
    got2 = lax.ppermute(send2, "date", [(i, (i + 1 ^ 1) - 1) for i in range(1, group - 1)])
    s01, s10 = resample(True)
    looked = pair(0, s00, s10, s01, s11)
    reference = flood(after(reference, looked), 8)
    looked = pair(1, me_one, s10, got1, got2, s01, looked)
    reference = exchange(after(reference, looked), 4)
    relayed = lax.all_to_all(looked.reshape(group, -1, LANES), "date", 0, 0, tiled=True)
    reference = exchange(reference, 2)
    reference, relayed = lax.optimization_barrier((reference, relayed))
    other = lax.ppermute(reference, "date", [(i, i ^ 1) for i in range(group)])

    share = blocks // group
    coherence = call(
        assemble_body,
        shape((2, tiles, share, looks, 2 * group - 1), F32),
        [VMEM, VMEM],
        cost=(10**7, 10**6),
    )(jnp.asarray(pair_places(group, share)), relayed.reshape(blocks, LANES))
    coherence = coherence.transpose(0, 4, 1, 2, 3)

    here = correlate(False, reference)
    there = correlate(True, other)
    half = me & 1
    half_chips = piece * near // 2 // CHIP
    low = jnp.where(half == 0, here, there).reshape(4, 16, LANES)[:, :half_chips, :2]
    high = jnp.where(half == 0, there, here).reshape(4, 16, LANES)[:, : chips - half_chips, :2]
    chip_corr = jnp.concatenate([low, high], axis=1).reshape(dates, tiles, chips_az, chips_rg, 2)
    return chip_corr.transpose(4, 0, 1, 2, 3), coherence


def solution(mesh):
    return jax.shard_map(
        per_device,
        mesh=mesh,
        in_specs=(
            P("date", None, None, None, "strip"),
            P(None, "date", None, None, "strip"),
            P(None, "date", None, None, "strip"),
            P(),
        ),
        out_specs=(P(None, "date", None, None, "strip"), P(None, None, None, "date", "strip")),
        check_vma=False,
    )
```

```python
import functools

import jax
import jax.numpy as jnp
import numpy as np
from jax import lax
from jax.experimental import pallas as pl
from jax.experimental.pallas import tpu as pltpu
from jax.sharding import PartitionSpec as P

CHIP = 64
TAPS = 8
SUBSTEPS = 64
MAX_SHIFT = 8
LOOK_AZ = 5
LOOK_RG = 20
MARGIN = 12
WINDOW = CHIP + 2 * MARGIN
LANES = 128
EDGE = 16
SKEW = 16
PACK = 16
EPSILON = 1e-06

VMEM = pl.BlockSpec(memory_space=pltpu.VMEM)
SMEM = pl.BlockSpec(memory_space=pltpu.SMEM)
F32 = jnp.float32
BF16 = jnp.bfloat16


def tap_table():
    x = np.arange(TAPS)[None, :] - (TAPS // 2 - 1) - np.arange(SUBSTEPS)[:, None] / SUBSTEPS
    weights = np.sinc(x) * (0.5 + 0.5 * np.cos(2 * np.pi * x / TAPS))
    weights = weights / weights.sum(axis=1, keepdims=True)
    table = np.zeros((SUBSTEPS, SKEW, LANES), np.float32)
    for line in range(SKEW):
        table[:, line, line : line + TAPS] = weights
    return table.astype(jnp.bfloat16)


def look_matrices(lines):
    chips = lines // CHIP
    looks = lines // LOOK_AZ
    plain = np.zeros((looks, chips, 2, CHIP), np.float32)
    for line in range(lines):
        plain[line // LOOK_AZ, line // CHIP, :, line % CHIP] = 1.0
    signed = plain.copy()
    signed[:, :, 1] *= -1.0
    return [m.reshape(looks, chips * LANES).astype(jnp.bfloat16) for m in (plain, signed)]


def lane_index(shape):
    return lax.broadcasted_iota(jnp.int32, shape, len(shape) - 1)


def call(body, outs, in_specs, scratch=(), cost=(0, 0)):
    return pl.pallas_call(
        body,
        out_shape=outs,
        in_specs=in_specs,
        out_specs=VMEM,
        scratch_shapes=list(scratch),
        cost_estimate=pl.CostEstimate(flops=cost[0], bytes_accessed=cost[1], transcendentals=0),
        compiler_params=pltpu.CompilerParams(vmem_limit_bytes=24 << 20),
    )


def lane_tiles(read, lines, stage):
    whole = lines // LANES
    stage[:, 0 : lines - whole * LANES] = read(slice(whole * LANES, lines))
    return [read(slice(k * LANES, (k + 1) * LANES)) for k in range(whole)] + [stage[...]]


def candidate_body(dates_ref, me_ref, x_ref, out_ref, stage):
    cols, lines = x_ref.shape[-2:]
    chips_az = (lines - 2 * MARGIN) // CHIP
    lane = lane_index((cols, LANES))
    parts = [lane_tiles(lambda part, p=p: x_ref[0, 0, p, :, part], lines, stage.at[p]) for p in range(2)]
    for a in range(chips_az):
        start = MARGIN + a * CHIP
        tile, offset = start // LANES, start % LANES
        halves = []
        for p in range(2):
            shift = (p * CHIP - offset) % LANES
            value = pltpu.roll(parts[p][tile], shift, 1)
            if offset + CHIP > LANES:
                value = jnp.where(lane < p * CHIP + LANES - offset, value, pltpu.roll(parts[p][tile + 1], shift, 1))
            halves.append(value)
        value = jnp.where(lane < CHIP, halves[0], halves[1])
        out_ref[a * cols : (a + 1) * cols, :] = value
    filled = chips_az * cols
    out_ref[filled:, :] = jnp.zeros((out_ref.shape[0] - filled, LANES), BF16)


def resample_body(crossed, me_ref, move_ref, table_ref, x_ref, left_ref, right_ref, *rest):
    out_refs = rest[: 2 if crossed else 4]
    stage, window, chips_ref = rest[len(out_refs) :]
    date = pl.program_id(0)
    t = 1 - date if crossed else date
    cols, lines = x_ref.shape[-2:]
    chips_az = (lines - 2 * MARGIN) // CHIP
    chips_rg = cols // CHIP
    depth = CHIP + 2 * EDGE

    def fill(read, count, scratch, at):
        lane = lane_index((count, LANES))
        for p in range(2):
            tiles = lane_tiles(functools.partial(read, p), lines, scratch.at[p])
            turned = [pltpu.roll(tile, CHIP, 1) for tile in tiles]
            for a in range(chips_az):
                tile = tiles[a // 2]
                if a % 2:
                    tile = jnp.where(lane < CHIP, turned[a // 2], turned[a // 2 + 1])
                window[a, p, at : at + count, :] = tile

    def left(p, part):
        return left_ref[0, 0, p, :, part]

    def right(p, part):
        return right_ref[0, 0, p, :, part]

    for p in range(2):
        stage[p, :, :] = jnp.zeros(stage.shape[1:], BF16)
    fill(left, EDGE, stage.at[:, 0:EDGE], 0)
    fill(lambda p, part: x_ref[0, 0, p, :, part], cols, stage, EDGE)
    fill(right, EDGE, stage.at[:, 0:EDGE], EDGE + cols)
    half = lane_index((depth, LANES)) < CHIP

    def skewed(move, offset):
        offset = offset - MAX_SHIFT + lax.div(move, SUBSTEPS)
        base = table_ref[lax.rem(move, SUBSTEPS)]
        return jnp.concatenate([pltpu.roll(base, offset + k, 1) for k in range(0, CHIP, SKEW)], axis=0)

    for r in range(chips_rg):
        start = r * CHIP
        firsts = []
        for a in range(chips_az):
            azimuth = skewed(move_ref[0, date, a, t, r], 9)
            both = jnp.concatenate([azimuth, azimuth], axis=0)
            data = jnp.concatenate([window[a, p, start : start + depth, :] for p in range(2)], axis=0)
            partial = lax.dot_general(data, both, (((1,), (1,)), ((), ())), preferred_element_type=F32)
            firsts.append(jnp.where(half, partial[:depth], partial[depth:]).astype(BF16))
        if r:
            for a in range(chips_az):
                across = skewed(move_ref[1, date, a, t, r - 1], 13)
                chip = jnp.dot(across[:, :depth], before[a], preferred_element_type=F32)
                chips_ref[a * cols + start - CHIP : a * cols + start, :] = chip.astype(BF16)
        before = firsts
    for a in range(chips_az):
        across = skewed(move_ref[1, date, a, t, r], 13)
        chip = jnp.dot(across[:, :depth], before[a], preferred_element_type=F32)
        chips_ref[a * cols + start : a * cols + start + CHIP, :] = chip.astype(BF16)

    for d in range(2):

        @pl.when(date == d)
        def _(d=d):
            out_refs[d][...] = chips_ref[...]

    if not crossed:
        parity = lax.rem(me_ref[0], 2)
        for side in range(2):

            @pl.when((date + parity + side) % 2 == 1)
            def _(side=side):
                out_refs[2 + side][...] = chips_ref[...]


def resample_call(crossed, me, moves, table, images, edges):
    dates, tiles, parts, cols, rows = images.shape
    chips_az = (rows - 2 * MARGIN) // CHIP
    lines = chips_az * cols

    count = 2 if crossed else 4

    def of_tile(date):
        return (date, 1 - date if crossed else date, 0, 0, 0)

    edge = pl.BlockSpec((1, 1, parts, EDGE, rows), of_tile)
    return pl.pallas_call(
        functools.partial(resample_body, crossed),
        out_shape=[jax.ShapeDtypeStruct((lines, LANES), BF16)] * count,
        grid=(dates,),
        in_specs=[
            SMEM,
            SMEM,
            pl.BlockSpec(table.shape, lambda date: (0, 0, 0)),
            pl.BlockSpec((1, 1, parts, cols, rows), of_tile),
            edge,
            edge,
        ],
        out_specs=[pl.BlockSpec((lines, LANES), lambda date: (0, 0))] * count,
        scratch_shapes=[
            pltpu.VMEM((parts, cols, LANES), BF16),
            pltpu.VMEM((chips_az, parts, cols + 2 * EDGE, LANES), BF16),
            pltpu.VMEM((lines, LANES), BF16),
        ],
        cost_estimate=pl.CostEstimate(
            flops=tiles * lines * 128 * 256 * 4, bytes_accessed=16 * rows * cols, transcendentals=0
        ),
        compiler_params=pltpu.CompilerParams(vmem_limit_bytes=16 << 20),
    )(me, moves, table, images, *edges)


def pair_body(pair, plain_ref, signed_ref, *rest):
    if pair == 1:
        me_ref, first_0, got1, got2, second_1, before_ref, out_ref, product, looked = rest
        even = lax.rem(me_ref[0], 2) == 0
        sources = [
            (lambda rows: first_0[rows, :], lambda rows: jnp.where(even, got1[rows, :], got2[rows, :])),
            (lambda rows: jnp.where(even, got2[rows, :], got1[rows, :]), lambda rows: second_1[rows, :]),
        ]
    else:
        first_0, second_0, first_1, second_1, out_ref, product, looked = rest
        sources = [
            (lambda rows: first_0[rows, :], lambda rows: second_0[rows, :]),
            (lambda rows: first_1[rows, :], lambda rows: second_1[rows, :]),
        ]
    chips_az = plain_ref.shape[1] // LANES
    cols = first_0.shape[0] // chips_az
    looks = cols // LOOK_RG
    for t, (read_first, read_second) in enumerate(sources):
        for a in range(chips_az):
            first = read_first(slice(a * cols, (a + 1) * cols)).astype(F32)
            second = read_second(slice(a * cols, (a + 1) * cols)).astype(F32)
            work = product.at[a % 2]
            work[0] = first * second
            work[1] = pltpu.roll(first, CHIP, 1) * second
            work[2] = first * first
            work[3] = second * second
            for q in range(4):
                total = work[q, pl.ds(0, looks, stride=LOOK_RG), :]
                for k in range(1, LOOK_RG):
                    total = total + work[q, pl.ds(k, looks, stride=LOOK_RG), :]
                row = (q * 2 + t) * looks
                looked[row : row + looks, a * LANES : (a + 1) * LANES] = total

    value = looked[...]
    top = value.astype(BF16)
    low = (value - top.astype(F32)).astype(BF16)

    def line_sums(matrix_ref):
        dims = (((1,), (1,)), ((), ()))
        matrix = matrix_ref[...]
        return lax.dot_general(matrix, top, dims, preferred_element_type=F32) + lax.dot_general(
            matrix, low, dims, preferred_element_type=F32
        )

    plain = line_sums(plain_ref)
    signed = line_sums(signed_ref)
    lane = lane_index(plain.shape)
    real = lane < LANES // 4
    by_32, by_64, by_96 = (pltpu.roll(plain, k, 1) for k in (32, 64, 96))
    power_first = jnp.where(real, by_64, by_96)
    power_second = jnp.where(real, by_32, by_64)
    value = jnp.where(real, plain, signed) / jnp.sqrt((power_first + EPSILON) * (power_second + EPSILON))
    if pair == 1:
        value = jnp.where(lane < CHIP, before_ref[...], pltpu.roll(value, CHIP, 1))
    out_ref[...] = value


def pair_places(group, blocks):
    places = np.zeros((group, blocks, blocks, 3, LANES), np.float32)
    for device in range(group):
        for block in range(blocks):
            for kind, p in enumerate((2 * device, 2 * device + 1, 2 * device - 1)):
                if 0 <= p < 2 * group - 1:
                    places[device, block, block, kind, p] = 1.0
    return places.reshape(group * blocks, blocks * 3 * LANES)


def assemble_body(places_ref, looked_ref, out_ref):
    pairs = out_ref.shape[-1]
    looks = out_ref.shape[-2]
    rows = jnp.transpose(looked_ref[...])
    spread = jnp.dot(rows, places_ref[...], precision=lax.Precision.HIGHEST, preferred_element_type=F32)
    for q in range(2):
        for t in range(2):
            low = (q * 2 + t) * looks
            for b in range(out_ref.shape[2]):
                at = b * 3 * LANES
                inner = spread[low : low + looks, at : at + LANES]
                at += (1 + t) * LANES
                outer = spread[CHIP + low : CHIP + low + looks, at : at + LANES]
                out_ref[q, t, b] = (inner + outer)[:, :pairs]


def correlate_body(other, me_ref, ref_ref, s00_ref, s01_ref, s10_ref, s11_ref, out_ref, sums):
    half_chips = ref_ref.shape[1] // CHIP
    chips = s00_ref.shape[0] // CHIP
    half = lax.rem(me_ref[0], 2)
    base = (1 - half if other else half) * half_chips
    lane = lane_index((8, LANES))
    sign = jnp.where(lane < CHIP, 1.0, -1.0)

    def fold(value):
        total = value[0:8]
        for k in range(1, CHIP // 8):
            total = total + value[8 * k : 8 * k + 8]
        return total

    def total(value):
        return jnp.sum(fold(value), axis=0, keepdims=True)

    for t in range(2):
        for k in range(half_chips):
            source = pl.multiple_of(jnp.minimum(base + k, chips - 1) * CHIP, CHIP)
            ref = ref_ref[t, k * CHIP : (k + 1) * CHIP, :].astype(F32)
            turned = pltpu.roll(ref, CHIP, 1)
            power = total(ref * ref)
            for d in range(2):
                s_ref = ((s00_ref, s01_ref), (s10_ref, s11_ref))[d][t]
                sec = s_ref[pl.ds(source, CHIP), :].astype(F32)
                at = (d * 2 + t) * 16 + k
                sums[0, at : at + 1, :] = total(ref * sec)
                sums[1, at : at + 1, :] = jnp.sum(fold(turned * sec) * sign, axis=0, keepdims=True)
                sums[2, at : at + 1, :] = total(sec * sec)
                sums[3, at : at + 1, :] = power
        for d in range(2):
            at = (d * 2 + t) * 16 + half_chips
            sums[:, at : at + 16 - half_chips, :] = jnp.zeros((4, 16 - half_chips, LANES), F32)
    real, imag, sec_power, ref_power = (jnp.sum(sums[q], axis=1, keepdims=True) for q in range(4))
    denominator = jnp.sqrt((ref_power + EPSILON) * (sec_power + EPSILON))
    wide = lane_index(out_ref.shape)
    out_ref[...] = jnp.where(wide == 0, real, imag) / denominator


def per_device(acquisitions, shifts, fractions, ref_dates):
    dates, tiles, parts, rows, cols = acquisitions.shape
    group = lax.axis_size("date")
    strips = lax.axis_size("strip")
    me = lax.axis_index("date")
    strip = lax.axis_index("strip")
    me_one = me.reshape(1).astype(jnp.int32)
    chips_az = (rows - 2 * MARGIN) // CHIP
    chips_rg = cols // CHIP
    chips = chips_az * chips_rg
    lines = chips * CHIP
    looks = cols // LOOK_RG
    blocks = chips_az * CHIP // LOOK_AZ
    near = 8
    piece = -(-lines // (near * 2 * PACK)) * 2 * PACK
    shape = jax.ShapeDtypeStruct
    image_bytes = rows * cols * 2
    images = acquisitions.transpose(0, 1, 2, 4, 3)
    moves = ((shifts + MAX_SHIFT) * SUBSTEPS + fractions).transpose(0, 1, 3, 2, 4)
    owners = ref_dates // dates

    table = jnp.asarray(tap_table())
    plain, signed = (jnp.asarray(m) for m in look_matrices(chips_az * CHIP))

    high_edge = images[:, :, :, cols - EDGE :]
    low_edge = images[:, :, :, :EDGE]
    even = strip % 2 == 0
    pairs1 = [(i, i ^ 1) for i in range(strips)]
    pairs2 = [(i, (i + 1 ^ 1) - 1) for i in range(1, strips - 1)]
    to_one, to_other = jnp.where(even, high_edge, low_edge), jnp.where(even, low_edge, high_edge)
    from_one = lax.ppermute(to_one, "strip", pairs1)
    from_other = lax.ppermute(to_other, "strip", pairs2)

    def after(value, *events):
        return lax.optimization_barrier((value, events))[0]

    def owned(step, dates_ref, me_ref):
        tile = (dates_ref[1] // dates == me_ref[0]).astype(jnp.int32)
        return (lax.rem(dates_ref[tile], dates), tile, 0, 0, 0)

    candidate = pl.pallas_call(
        candidate_body,
        out_shape=shape((piece * near, LANES), BF16),
        grid_spec=pltpu.PrefetchScalarGridSpec(
            num_scalar_prefetch=2,
            grid=(1,),
            in_specs=[pl.BlockSpec((1, 1, parts, cols, rows), owned)],
            out_specs=pl.BlockSpec((piece * near, LANES), lambda *_: (0, 0)),
            scratch_shapes=[pltpu.VMEM((parts, cols, LANES), BF16)],
        ),
        cost_estimate=pl.CostEstimate(flops=10**6, bytes_accessed=4 * image_bytes, transcendentals=0),
        compiler_params=pltpu.CompilerParams(vmem_limit_bytes=60 << 20),
    )(after(ref_dates, to_one, to_other), me_one, images)
    reference = jnp.stack([candidate] * tiles)
    step = 1
    while step < near:
        halves = reference.reshape(tiles, 2, -1, LANES)
        high = (me & step) != 0
        own = jnp.where(high, halves[:, 1], halves[:, 0])
        away = jnp.where(high, halves[:, 0], halves[:, 1])
        if step == 1:
            away = away[0]
        other = lax.ppermute(away, "date", [(i, i ^ step) for i in range(group)])
        same = ((me ^ owners) & step) == 0
        reference = jnp.where(same[:, None, None], own, other if step > 1 else other[None])
        step *= 2

    edges = (jnp.where(even, from_other, from_one), jnp.where(even, from_one, from_other))

    resample = functools.partial(resample_call, me=me_one, moves=moves, table=table, images=images, edges=edges)

    def pair(index, *values):
        return call(
            functools.partial(pair_body, index),
            shape((blocks, LANES), F32),
            [VMEM] * 2 + [SMEM] * index + [VMEM] * (len(values) - index),
            [
                pltpu.VMEM((2, 4, cols, LANES), F32),
                pltpu.VMEM((4 * tiles * looks, chips_az * LANES), F32),
            ],
            cost=(10**8, 8 * image_bytes),
        )(plain, signed, *values)

    def correlate(other, value):
        return call(
            functools.partial(correlate_body, other),
            shape((4 * 16, LANES), F32),
            [SMEM] + [VMEM] * 5,
            [pltpu.VMEM((4, 4 * 16, LANES), F32)],
            cost=(10**7, 3 * image_bytes),
        )(me_one, value.reshape(tiles, -1, LANES), s00, s01, s10, s11)

    def exchange(value, step):
        other = lax.ppermute(value, "date", [(i, i ^ step) for i in range(group)])
        high = (me & step) != 0
        return jnp.concatenate([jnp.where(high, other, value), jnp.where(high, value, other)], axis=1)

    def flood(value, step):
        other = lax.ppermute(value, "date", [(i, i ^ step) for i in range(group)])
        same = ((me ^ owners) & step) == 0
        return jnp.where(same[:, None, None], value, other)

    reference = flood(reference, 16)
    s00, s11, send1, send2 = resample(False)
    got1 = lax.ppermute(send1, "date", [(i, i ^ 1) for i in range(group)])
    got2 = lax.ppermute(send2, "date", [(i, (i + 1 ^ 1) - 1) for i in range(1, group - 1)])
    reference = flood(after(reference, s00), 8)
    s01, s10 = resample(True)
    looked = pair(0, s00, s10, s01, s11)
    reference = exchange(after(reference, looked), 4)
    looked = pair(1, me_one, s10, got1, got2, s01, looked)
    relayed = lax.all_to_all(looked.reshape(group, -1, LANES), "date", 0, 0, tiled=True)
    reference = exchange(after(reference, looked), 2)
    reference, relayed = lax.optimization_barrier((reference, relayed))
    other = lax.ppermute(reference, "date", [(i, i ^ 1) for i in range(group)])

    share = blocks // group
    coherence = call(
        assemble_body,
        shape((2, tiles, share, looks, 2 * group - 1), F32),
        [VMEM, VMEM],
        cost=(10**7, 10**6),
    )(jnp.asarray(pair_places(group, share)), relayed.reshape(blocks, LANES))
    coherence = coherence.transpose(0, 4, 1, 2, 3)

    here = correlate(False, reference)
    there = correlate(True, other)
    half = me & 1
    half_chips = piece * near // 2 // CHIP
    low = jnp.where(half == 0, here, there).reshape(4, 16, LANES)[:, :half_chips, :2]
    high = jnp.where(half == 0, there, here).reshape(4, 16, LANES)[:, : chips - half_chips, :2]
    chip_corr = jnp.concatenate([low, high], axis=1).reshape(dates, tiles, chips_az, chips_rg, 2)
    return chip_corr.transpose(4, 0, 1, 2, 3), coherence


def solution(mesh):
    return jax.shard_map(
        per_device,
        mesh=mesh,
        in_specs=(
            P("date", None, None, None, "strip"),
            P(None, "date", None, None, "strip"),
            P(None, "date", None, None, "strip"),
            P(),
        ),
        out_specs=(P(None, "date", None, None, "strip"), P(None, None, None, "date", "strip")),
        check_vma=False,
    )
```

```python
import functools

import jax
import jax.numpy as jnp
import numpy as np
from jax import lax
from jax.experimental import pallas as pl
from jax.experimental.pallas import tpu as pltpu
from jax.sharding import PartitionSpec as P

CHIP = 64
TAPS = 8
SUBSTEPS = 64
MAX_SHIFT = 8
LOOK_AZ = 5
LOOK_RG = 20
MARGIN = 12
WINDOW = CHIP + 2 * MARGIN
LANES = 128
EDGE = 16
SKEW = 16
PACK = 16
EPSILON = 1e-06

VMEM = pl.BlockSpec(memory_space=pltpu.VMEM)
SMEM = pl.BlockSpec(memory_space=pltpu.SMEM)
F32 = jnp.float32
BF16 = jnp.bfloat16


def tap_table():
    x = np.arange(TAPS)[None, :] - (TAPS // 2 - 1) - np.arange(SUBSTEPS)[:, None] / SUBSTEPS
    weights = np.sinc(x) * (0.5 + 0.5 * np.cos(2 * np.pi * x / TAPS))
    weights = weights / weights.sum(axis=1, keepdims=True)
    table = np.zeros((SUBSTEPS, SKEW, LANES), np.float32)
    for line in range(SKEW):
        table[:, line, line : line + TAPS] = weights
    return table.astype(jnp.bfloat16)


def look_matrices(lines):
    chips = lines // CHIP
    looks = lines // LOOK_AZ
    plain = np.zeros((looks, chips, 2, CHIP), np.float32)
    for line in range(lines):
        plain[line // LOOK_AZ, line // CHIP, :, line % CHIP] = 1.0
    signed = plain.copy()
    signed[:, :, 1] *= -1.0
    return [m.reshape(looks, chips * LANES).astype(jnp.bfloat16) for m in (plain, signed)]


def lane_index(shape):
    return lax.broadcasted_iota(jnp.int32, shape, len(shape) - 1)


def call(body, outs, in_specs, scratch=(), cost=(0, 0)):
    return pl.pallas_call(
        body,
        out_shape=outs,
        in_specs=in_specs,
        out_specs=VMEM,
        scratch_shapes=list(scratch),
        cost_estimate=pl.CostEstimate(flops=cost[0], bytes_accessed=cost[1], transcendentals=0),
        compiler_params=pltpu.CompilerParams(vmem_limit_bytes=24 << 20),
    )


def reversed_bits(value, count):
    result = 0
    while count > 1:
        result = result * 2 + value % 2
        value //= 2
        count //= 2
    return result


def lane_tiles(read, lines, stage):
    whole = lines // LANES
    stage[:, 0 : lines - whole * LANES] = read(slice(whole * LANES, lines))
    return [read(slice(k * LANES, (k + 1) * LANES)) for k in range(whole)] + [stage[...]]


def candidate_body(group, dates_ref, me_ref, x_ref, out_ref, stage):
    cols, lines = x_ref.shape[-2:]
    chips_az = (lines - 2 * MARGIN) // CHIP
    lane = lane_index((cols, LANES))
    steps = out_ref.shape[0] // PACK // group

    def place(step):
        return (reversed_bits(step // steps, group) * steps + step % steps) * PACK

    parts = [lane_tiles(lambda part, p=p: x_ref[0, 0, p, :, part], lines, stage.at[p]) for p in range(2)]
    for a in range(chips_az):
        start = MARGIN + a * CHIP
        tile, offset = start // LANES, start % LANES
        halves = []
        for p in range(2):
            shift = (p * CHIP - offset) % LANES
            value = pltpu.roll(parts[p][tile], shift, 1)
            if offset + CHIP > LANES:
                value = jnp.where(lane < p * CHIP + LANES - offset, value, pltpu.roll(parts[p][tile + 1], shift, 1))
            halves.append(value)
        value = jnp.where(lane < CHIP, halves[0], halves[1])
        for k in range(cols // PACK):
            at = place(a * (cols // PACK) + k)
            out_ref[at : at + PACK, :] = value[PACK * k : PACK * (k + 1)]
    for step in range(chips_az * cols // PACK, out_ref.shape[0] // PACK):
        at = place(step)
        out_ref[at : at + PACK, :] = jnp.zeros((PACK, LANES), BF16)


def resample_body(crossed, me_ref, move_ref, table_ref, x_ref, left_ref, right_ref, *rest):
    out_refs = rest[: 2 if crossed else 4]
    stage, window, chips_ref = rest[len(out_refs) :]
    date = pl.program_id(0)
    t = 1 - date if crossed else date
    cols, lines = x_ref.shape[-2:]
    chips_az = (lines - 2 * MARGIN) // CHIP
    chips_rg = cols // CHIP
    depth = CHIP + 2 * EDGE

    def fill(read, count, scratch, at):
        lane = lane_index((count, LANES))
        for p in range(2):
            tiles = lane_tiles(functools.partial(read, p), lines, scratch.at[p])
            turned = [pltpu.roll(tile, CHIP, 1) for tile in tiles]
            for a in range(chips_az):
                tile = tiles[a // 2]
                if a % 2:
                    tile = jnp.where(lane < CHIP, turned[a // 2], turned[a // 2 + 1])
                window[a, p, at : at + count, :] = tile

    def left(p, part):
        return left_ref[0, 0, p, :, part]

    def right(p, part):
        return right_ref[0, 0, p, :, part]

    for p in range(2):
        stage[p, :, :] = jnp.zeros(stage.shape[1:], BF16)
    fill(left, EDGE, stage.at[:, 0:EDGE], 0)
    fill(lambda p, part: x_ref[0, 0, p, :, part], cols, stage, EDGE)
    fill(right, EDGE, stage.at[:, 0:EDGE], EDGE + cols)
    half = lane_index((depth, LANES)) < CHIP

    def skewed(move, offset):
        offset = offset - MAX_SHIFT + lax.div(move, SUBSTEPS)
        base = table_ref[lax.rem(move, SUBSTEPS)]
        return jnp.concatenate([pltpu.roll(base, offset + k, 1) for k in range(0, CHIP, SKEW)], axis=0)

    for r in range(chips_rg):
        start = r * CHIP
        firsts = []
        for a in range(chips_az):
            azimuth = skewed(move_ref[0, date, a, t, r], 9)
            both = jnp.concatenate([azimuth, azimuth], axis=0)
            data = jnp.concatenate([window[a, p, start : start + depth, :] for p in range(2)], axis=0)
            partial = lax.dot_general(data, both, (((1,), (1,)), ((), ())), preferred_element_type=F32)
            firsts.append(jnp.where(half, partial[:depth], partial[depth:]).astype(BF16))
        if r:
            for a in range(chips_az):
                across = skewed(move_ref[1, date, a, t, r - 1], 13)
                chip = jnp.dot(across[:, :depth], before[a], preferred_element_type=F32)
                chips_ref[a * cols + start - CHIP : a * cols + start, :] = chip.astype(BF16)
        before = firsts
    for a in range(chips_az):
        across = skewed(move_ref[1, date, a, t, r], 13)
        chip = jnp.dot(across[:, :depth], before[a], preferred_element_type=F32)
        chips_ref[a * cols + start : a * cols + start + CHIP, :] = chip.astype(BF16)

    for d in range(2):

        @pl.when(date == d)
        def _(d=d):
            out_refs[d][...] = chips_ref[...]

    if not crossed:
        parity = lax.rem(me_ref[0], 2)
        for side in range(2):

            @pl.when((date + parity + side) % 2 == 1)
            def _(side=side):
                out_refs[2 + side][...] = chips_ref[...]


def resample_call(crossed, me, moves, table, images, edges):
    dates, tiles, parts, cols, rows = images.shape
    chips_az = (rows - 2 * MARGIN) // CHIP
    lines = chips_az * cols

    count = 2 if crossed else 4

    def of_tile(date):
        return (date, 1 - date if crossed else date, 0, 0, 0)

    edge = pl.BlockSpec((1, 1, parts, EDGE, rows), of_tile)
    return pl.pallas_call(
        functools.partial(resample_body, crossed),
        out_shape=[jax.ShapeDtypeStruct((lines, LANES), BF16)] * count,
        grid=(dates,),
        in_specs=[
            SMEM,
            SMEM,
            pl.BlockSpec(table.shape, lambda date: (0, 0, 0)),
            pl.BlockSpec((1, 1, parts, cols, rows), of_tile),
            edge,
            edge,
        ],
        out_specs=[pl.BlockSpec((lines, LANES), lambda date: (0, 0))] * count,
        scratch_shapes=[
            pltpu.VMEM((parts, cols, LANES), BF16),
            pltpu.VMEM((chips_az, parts, cols + 2 * EDGE, LANES), BF16),
            pltpu.VMEM((lines, LANES), BF16),
        ],
        cost_estimate=pl.CostEstimate(
            flops=tiles * lines * 128 * 256 * 4, bytes_accessed=16 * rows * cols, transcendentals=0
        ),
        compiler_params=pltpu.CompilerParams(vmem_limit_bytes=16 << 20),
    )(me, moves, table, images, *edges)


def pair_body(pair, plain_ref, signed_ref, *rest):
    if pair == 1:
        me_ref, first_0, got1, got2, second_1, before_ref, out_ref, product, looked = rest
        even = lax.rem(me_ref[0], 2) == 0
        sources = [
            (lambda rows: first_0[rows, :], lambda rows: jnp.where(even, got1[rows, :], got2[rows, :])),
            (lambda rows: jnp.where(even, got2[rows, :], got1[rows, :]), lambda rows: second_1[rows, :]),
        ]
    else:
        first_0, second_0, first_1, second_1, out_ref, product, looked = rest
        sources = [
            (lambda rows: first_0[rows, :], lambda rows: second_0[rows, :]),
            (lambda rows: first_1[rows, :], lambda rows: second_1[rows, :]),
        ]
    chips_az = plain_ref.shape[1] // LANES
    cols = first_0.shape[0] // chips_az
    looks = cols // LOOK_RG
    for t, (read_first, read_second) in enumerate(sources):
        for a in range(chips_az):
            first = read_first(slice(a * cols, (a + 1) * cols)).astype(F32)
            second = read_second(slice(a * cols, (a + 1) * cols)).astype(F32)
            work = product.at[a % 2]
            work[0] = first * second
            work[1] = pltpu.roll(first, CHIP, 1) * second
            work[2] = first * first
            work[3] = second * second
            for q in range(4):
                total = work[q, pl.ds(0, looks, stride=LOOK_RG), :]
                for k in range(1, LOOK_RG):
                    total = total + work[q, pl.ds(k, looks, stride=LOOK_RG), :]
                row = (q * 2 + t) * looks
                looked[row : row + looks, a * LANES : (a + 1) * LANES] = total

    value = looked[...]
    top = value.astype(BF16)
    low = (value - top.astype(F32)).astype(BF16)

    def line_sums(matrix_ref):
        dims = (((1,), (1,)), ((), ()))
        matrix = matrix_ref[...]
        return lax.dot_general(matrix, top, dims, preferred_element_type=F32) + lax.dot_general(
            matrix, low, dims, preferred_element_type=F32
        )

    plain = line_sums(plain_ref)
    signed = line_sums(signed_ref)
    lane = lane_index(plain.shape)
    real = lane < LANES // 4
    by_32, by_64, by_96 = (pltpu.roll(plain, k, 1) for k in (32, 64, 96))
    power_first = jnp.where(real, by_64, by_96)
    power_second = jnp.where(real, by_32, by_64)
    value = jnp.where(real, plain, signed) / jnp.sqrt((power_first + EPSILON) * (power_second + EPSILON))
    if pair == 1:
        value = jnp.where(lane < CHIP, before_ref[...], pltpu.roll(value, CHIP, 1))
    out_ref[...] = value


def pair_places(group, blocks):
    places = np.zeros((group, blocks, blocks, 3, LANES), np.float32)
    for device in range(group):
        for block in range(blocks):
            for kind, p in enumerate((2 * device, 2 * device + 1, 2 * device - 1)):
                if 0 <= p < 2 * group - 1:
                    places[device, block, block, kind, p] = 1.0
    return places.reshape(group * blocks, blocks * 3 * LANES)


def assemble_body(places_ref, looked_ref, out_ref):
    pairs = out_ref.shape[-1]
    looks = out_ref.shape[-2]
    rows = jnp.transpose(looked_ref[...])
    spread = jnp.dot(rows, places_ref[...], precision=lax.Precision.HIGHEST, preferred_element_type=F32)
    for q in range(2):
        for t in range(2):
            low = (q * 2 + t) * looks
            for b in range(out_ref.shape[2]):
                at = b * 3 * LANES
                inner = spread[low : low + looks, at : at + LANES]
                at += (1 + t) * LANES
                outer = spread[CHIP + low : CHIP + low + looks, at : at + LANES]
                out_ref[q, t, b] = (inner + outer)[:, :pairs]


def correlate_body(other, me_ref, ref_ref, s00_ref, s01_ref, s10_ref, s11_ref, out_ref, sums):
    half_chips = ref_ref.shape[1] // CHIP
    chips = s00_ref.shape[0] // CHIP
    half = lax.rem(me_ref[0], 2)
    base = (1 - half if other else half) * half_chips
    lane = lane_index((8, LANES))
    sign = jnp.where(lane < CHIP, 1.0, -1.0)

    def fold(value):
        total = value[0:8]
        for k in range(1, CHIP // 8):
            total = total + value[8 * k : 8 * k + 8]
        return total

    def total(value):
        return jnp.sum(fold(value), axis=0, keepdims=True)

    for t in range(2):
        for k in range(half_chips):
            source = pl.multiple_of(jnp.minimum(base + k, chips - 1) * CHIP, CHIP)
            ref = ref_ref[t, k * CHIP : (k + 1) * CHIP, :].astype(F32)
            turned = pltpu.roll(ref, CHIP, 1)
            power = total(ref * ref)
            for d in range(2):
                s_ref = ((s00_ref, s01_ref), (s10_ref, s11_ref))[d][t]
                sec = s_ref[pl.ds(source, CHIP), :].astype(F32)
                at = (d * 2 + t) * 16 + k
                sums[0, at : at + 1, :] = total(ref * sec)
                sums[1, at : at + 1, :] = jnp.sum(fold(turned * sec) * sign, axis=0, keepdims=True)
                sums[2, at : at + 1, :] = total(sec * sec)
                sums[3, at : at + 1, :] = power
        for d in range(2):
            at = (d * 2 + t) * 16 + half_chips
            sums[:, at : at + 16 - half_chips, :] = jnp.zeros((4, 16 - half_chips, LANES), F32)
    real, imag, sec_power, ref_power = (jnp.sum(sums[q], axis=1, keepdims=True) for q in range(4))
    denominator = jnp.sqrt((ref_power + EPSILON) * (sec_power + EPSILON))
    wide = lane_index(out_ref.shape)
    out_ref[...] = jnp.where(wide == 0, real, imag) / denominator


def per_device(acquisitions, shifts, fractions, ref_dates):
    dates, tiles, parts, rows, cols = acquisitions.shape
    group = lax.axis_size("date")
    strips = lax.axis_size("strip")
    me = lax.axis_index("date")
    strip = lax.axis_index("strip")
    me_one = me.reshape(1).astype(jnp.int32)
    chips_az = (rows - 2 * MARGIN) // CHIP
    chips_rg = cols // CHIP
    chips = chips_az * chips_rg
    lines = chips * CHIP
    looks = cols // LOOK_RG
    blocks = chips_az * CHIP // LOOK_AZ
    near = 8
    piece = -(-lines // (near * 2 * PACK)) * 2 * PACK
    shape = jax.ShapeDtypeStruct
    image_bytes = rows * cols * 2
    images = acquisitions.transpose(0, 1, 2, 4, 3)
    moves = ((shifts + MAX_SHIFT) * SUBSTEPS + fractions).transpose(0, 1, 3, 2, 4)
    owners = ref_dates // dates

    table = jnp.asarray(tap_table())
    plain, signed = (jnp.asarray(m) for m in look_matrices(chips_az * CHIP))

    high_edge = images[:, :, :, cols - EDGE :]
    low_edge = images[:, :, :, :EDGE]
    even = strip % 2 == 0
    pairs1 = [(i, i ^ 1) for i in range(strips)]
    pairs2 = [(i, (i + 1 ^ 1) - 1) for i in range(1, strips - 1)]
    to_one, to_other = jnp.where(even, high_edge, low_edge), jnp.where(even, low_edge, high_edge)
    from_one = lax.ppermute(to_one, "strip", pairs1)
    from_other = lax.ppermute(to_other, "strip", pairs2)

    def after(value, *events):
        return lax.optimization_barrier((value, events))[0]

    def owned(step, dates_ref, me_ref):
        tile = (dates_ref[1] // dates == me_ref[0]).astype(jnp.int32)
        return (lax.rem(dates_ref[tile], dates), tile, 0, 0, 0)

    candidate = pl.pallas_call(
        functools.partial(candidate_body, near),
        out_shape=shape((piece * near, LANES), BF16),
        grid_spec=pltpu.PrefetchScalarGridSpec(
            num_scalar_prefetch=2,
            grid=(1,),
            in_specs=[pl.BlockSpec((1, 1, parts, cols, rows), owned)],
            out_specs=pl.BlockSpec((piece * near, LANES), lambda *_: (0, 0)),
            scratch_shapes=[pltpu.VMEM((parts, cols, LANES), BF16)],
        ),
        cost_estimate=pl.CostEstimate(flops=10**6, bytes_accessed=4 * image_bytes, transcendentals=0),
        compiler_params=pltpu.CompilerParams(vmem_limit_bytes=16 << 20),
    )(after(ref_dates, to_one, to_other), me_one, images)
    scattered = lax.all_to_all(
        candidate.reshape(near, piece, LANES),
        "date",
        0,
        0,
        axis_index_groups=[list(range(k, k + near)) for k in range(0, group, near)],
        tiled=True,
    )
    from_owner = jnp.arange(near)[None, :] == (owners % near)[:, None]
    reference = jnp.sum(jnp.where(from_owner[:, :, None, None], scattered[None], 0), axis=1, dtype=BF16)
    edges = (jnp.where(even, from_other, from_one), jnp.where(even, from_one, from_other))

    resample = functools.partial(resample_call, me=me_one, moves=moves, table=table, images=images, edges=edges)

    def pair(index, *values):
        return call(
            functools.partial(pair_body, index),
            shape((blocks, LANES), F32),
            [VMEM] * 2 + [SMEM] * index + [VMEM] * (len(values) - index),
            [
                pltpu.VMEM((2, 4, cols, LANES), F32),
                pltpu.VMEM((4 * tiles * looks, chips_az * LANES), F32),
            ],
            cost=(10**8, 8 * image_bytes),
        )(plain, signed, *values)

    def correlate(other, value):
        return call(
            functools.partial(correlate_body, other),
            shape((4 * 16, LANES), F32),
            [SMEM] + [VMEM] * 5,
            [pltpu.VMEM((4, 4 * 16, LANES), F32)],
            cost=(10**7, 3 * image_bytes),
        )(me_one, value.reshape(tiles, -1, LANES), s00, s01, s10, s11)

    def exchange(value, step):
        other = lax.ppermute(value, "date", [(i, i ^ step) for i in range(group)])
        high = (me & step) != 0
        return jnp.concatenate([jnp.where(high, other, value), jnp.where(high, value, other)], axis=1)

    def flood(value, step):
        other = lax.ppermute(value, "date", [(i, i ^ step) for i in range(group)])
        same = ((me ^ owners) & step) == 0
        return jnp.where(same[:, None, None], value, other)

    reference = flood(reference, 16)
    s00, s11, send1, send2 = resample(False)
    got1 = lax.ppermute(send1, "date", [(i, i ^ 1) for i in range(group)])
    got2 = lax.ppermute(send2, "date", [(i, (i + 1 ^ 1) - 1) for i in range(1, group - 1)])
    s01, s10 = resample(True)
    looked = pair(0, s00, s10, s01, s11)
    reference = flood(after(reference, looked), 8)
    looked = pair(1, me_one, s10, got1, got2, s01, looked)
    reference = exchange(after(reference, looked), 4)
    relayed = lax.all_to_all(looked.reshape(group, -1, LANES), "date", 0, 0, tiled=True)
    reference = exchange(reference, 2)
    reference, relayed = lax.optimization_barrier((reference, relayed))
    other = lax.ppermute(reference, "date", [(i, i ^ 1) for i in range(group)])

    share = blocks // group
    coherence = call(
        assemble_body,
        shape((2, tiles, share, looks, 2 * group - 1), F32),
        [VMEM, VMEM],
        cost=(10**7, 10**6),
    )(jnp.asarray(pair_places(group, share)), relayed.reshape(blocks, LANES))
    coherence = coherence.transpose(0, 4, 1, 2, 3)

    here = correlate(False, reference)
    there = correlate(True, other)
    half = me & 1
    half_chips = piece * near // 2 // CHIP
    low = jnp.where(half == 0, here, there).reshape(4, 16, LANES)[:, :half_chips, :2]
    high = jnp.where(half == 0, there, here).reshape(4, 16, LANES)[:, : chips - half_chips, :2]
    chip_corr = jnp.concatenate([low, high], axis=1).reshape(dates, tiles, chips_az, chips_rg, 2)
    return chip_corr.transpose(4, 0, 1, 2, 3), coherence


def solution(mesh):
    return jax.shard_map(
        per_device,
        mesh=mesh,
        in_specs=(
            P("date", None, None, None, "strip"),
            P(None, "date", None, None, "strip"),
            P(None, "date", None, None, "strip"),
            P(),
        ),
        out_specs=(P(None, "date", None, None, "strip"), P(None, None, None, "date", "strip")),
        check_vma=False,
    )
```
